32 devices in a mesh: dp: 8 (over z, x), tp: 4 (over y, core).
Axes of the slice: x: 2, y: 2, z: 4, core: 2. Of those that a mesh axis runs over, the one named last changes fastest.
Arguments:
- tokens: bfloat16 [8192, 512], P(('dp', 'tp')), may hold values from -6 to 6
- segment_ids: int32 [8192], P('dp'), may hold values from 0 to 8191, as said below
- out_grad: bfloat16 [8192, 512], P(('dp', 'tp')), may hold values from -6 to 6
- norm1_gain: float32 [512], replicated, may hold values from 0.5 to 1.5
- in_weight: bfloat16 [512, 2, 1024], P('dp', None, 'tp'), may hold values from -0.25 to 0.25
- conv_weight: float32 [4, 1024], P(None, 'tp'), may hold values from -3 to 3
- conv_bias: float32 [1024], P('tp'), may hold values from -3 to 3
- xproj_weight: bfloat16 [1024, 64], P('tp'), may hold values from -0.1875 to 0.1875
- dtproj_weight: bfloat16 [32, 1024], P(None, 'tp'), may hold values from -1 to 1
- dt_bias: float32 [1024], P('tp'), may hold values from -4.6 to -2.3
- a_log: float32 [1024, 16], P('tp'), may hold values from 0 to 2.77
- d_skip: float32 [1024], P('tp'), may hold values from 0.5 to 1.5
- out_weight: bfloat16 [512, 1024], P('dp', 'tp'), may hold values from -0.1875 to 0.1875
- norm2_gain: float32 [512], replicated, may hold values from 0.5 to 1.5
- qkv_weight: bfloat16 [512, 3, 512], P('dp', None, 'tp'), may hold values from -0.25 to 0.25
- attn_out_weight: bfloat16 [512, 512], P('dp', 'tp'), may hold values from -0.75 to 0.75
- norm3_gain: float32 [512], replicated, may hold values from 0.5 to 1.5
- up_weight: bfloat16 [512, 2048], P('dp', 'tp'), may hold values from -0.25 to 0.25
- down_weight: bfloat16 [512, 2048], P('dp', 'tp'), may hold values from -0.125 to 0.125
Outputs:
- result: bfloat16 [8192, 512], P(('dp', 'tp'))
- in_grad: float32 [8192, 512], P(('dp', 'tp'))
- norm1_gain_grad: float32 [512], replicated
- in_weight_grad: float32 [512, 2, 1024], P('dp', None, 'tp')
- conv_weight_grad: float32 [4, 1024], P(None, 'tp')
- conv_bias_grad: float32 [1024], P('tp')
- xproj_weight_grad: float32 [1024, 64], P('tp')
- dtproj_weight_grad: float32 [32, 1024], P(None, 'tp')
- dt_bias_grad: float32 [1024], P('tp')
- a_log_grad: float32 [1024, 16], P('tp')
- d_skip_grad: float32 [1024], P('tp')
- out_weight_grad: float32 [512, 1024], P('dp', 'tp')
- norm2_gain_grad: float32 [512], replicated
- qkv_weight_grad: float32 [512, 3, 512], P('dp', None, 'tp')
- attn_out_weight_grad: float32 [512, 512], P('dp', 'tp')
- norm3_gain_grad: float32 [512], replicated
- up_weight_grad: float32 [512, 2048], P('dp', 'tp')
- down_weight_grad: float32 [512, 2048], P('dp', 'tp')
The draws below stay inside these ranges and needn't reach their ends.
Inputs may be any that keep to these rules, and one draw needn't show every extreme that they name: `segment_ids`: segment numbers never fall along the tokens, the first token of each 1024-token sequence begins a new segment, and different documents have different numbers; the last document ends at the last token with number 8192 - 1.
All inputs are finite; a program needn't handle non-finite values.
Results may differ from the reference program's by a relative error of at most 0.02.
Values may be sent and summed in bfloat16 or wider, within the bound.
A program may use at most 128 MiB of HBM per device.

```python
import math
import jax
import jax.numpy as jnp
from jax import lax

D = 512
DI = 1024
NST = 16
RANK = 32
KC = 4
H = 8
HD = 64
FF = 2048
LEN = 1024
QBLK = 512
SBLK = 256
TOKENS = 8192


def draw_segment_ids(key, part):
    seq_count = TOKENS // LEN
    least_len = max(LEN * 60 // 1024, 1)
    most_len = LEN * 800 // 1024 + 1
    draws_per = LEN // least_len + 1
    lengths = jax.random.randint(key, (seq_count, draws_per), least_len, most_len)
    boundaries = jnp.cumsum(lengths, axis=1)
    positions = jnp.arange(LEN).astype(jnp.int32)
    starts_here = jnp.any(boundaries[:, :, None] == positions[None, None, :], axis=1)
    ends_here = jnp.concatenate([starts_here[:, 1:], jnp.ones((seq_count, 1), dtype=bool)], 1)
    marked = jnp.where(ends_here, positions[None, :], LEN).astype(jnp.int32)
    doc_end = lax.cummin(marked, axis=1, reverse=True)
    seq_base = (jnp.arange(seq_count).astype(jnp.int32) * LEN)[:, None]
    return (seq_base + doc_end).reshape(-1).astype(jnp.int32)


def level_of(rng, shape, cuts, low, largest):
    def one(axis_at, parts):
        steps = jax.random.uniform(jax.random.fold_in(jax.random.fold_in(rng, 6), axis_at), (parts,), jnp.float32, low / len(cuts), largest / len(cuts))
        return jnp.repeat(jnp.exp(steps), shape[axis_at] // parts).reshape((-1,) + (1,) * (len(shape) - axis_at - 1))

    level = one(*cuts[0])
    for cut in cuts[1:]:
        level = level * one(*cut)
    return level


def bell_draw(key, dims, width, most, cuts=(), kind=jnp.bfloat16):
    gain = level_of(key, dims, cuts, -0.22, 0.18) if cuts else 1.0
    drawn = jax.random.normal(key, dims, jnp.float32) * width * gain
    return jnp.minimum(jnp.maximum(drawn, -most), most).astype(kind)


def setup_inputs(seed: int = 0) -> dict:
    key_list = jax.random.split(jax.random.key(seed), 20)
    return {
        "tokens": bell_draw(key_list[0], (TOKENS, D), 1.0, 6.0, ((0, 32),)),
        "segment_ids": draw_segment_ids(jax.random.fold_in(key_list[19], 71), 0),
        "out_grad": bell_draw(key_list[2], (TOKENS, D), 1.0, 6.0, ((0, 32),)),
        "norm1_gain": jnp.clip(1.0 + 0.1 * jax.random.normal(key_list[3], (D,), jnp.float32), 0.5, 1.5),
        "in_weight": bell_draw(key_list[4], (D, 2, DI), D ** -0.5, 0.25, ((0, 8), (2, 4))),
        "conv_weight": bell_draw(key_list[5], (KC, DI), KC ** -0.5, 3.0, ((1, 4),), jnp.float32),
        "conv_bias": bell_draw(key_list[6], (DI,), 0.5, 3.0, ((0, 4),), jnp.float32),
        "xproj_weight": bell_draw(key_list[7], (DI, RANK + 2 * NST), DI ** -0.5, 0.1875, ((0, 4),)),
        "dtproj_weight": bell_draw(key_list[8], (RANK, DI), RANK ** -0.5, 1.0, ((1, 4),)),
        "dt_bias": jnp.clip(-4.6 + 2.3 * jax.random.uniform(key_list[9], (DI,), jnp.float32) ** level_of(key_list[9], (DI,), ((0, 4),), -0.2, 0.2), -4.6, -2.3),
        "a_log": jnp.clip(2.77 * jax.random.uniform(key_list[10], (DI, NST), jnp.float32) ** level_of(key_list[10], (DI, NST), ((0, 4),), -0.2, 0.2), 0.0, 2.77),
        "d_skip": jnp.clip(0.5 + 1.0 * jax.random.uniform(key_list[11], (DI,), jnp.float32) ** level_of(key_list[11], (DI,), ((0, 4),), -0.2, 0.2), 0.5, 1.5),
        "out_weight": bell_draw(key_list[12], (D, DI), DI ** -0.5, 0.1875, ((0, 8), (1, 4))),
        "norm2_gain": jnp.clip(1.0 + 0.1 * jax.random.normal(key_list[13], (D,), jnp.float32), 0.5, 1.5),
        "qkv_weight": bell_draw(key_list[14], (D, 3, H * HD), D ** -0.5, 0.25, ((0, 8), (2, 4))),
        "attn_out_weight": bell_draw(key_list[15], (D, H * HD), (H * HD // 8) ** -0.5, 0.75, ((0, 8), (1, 4))),
        "norm3_gain": jnp.clip(1.0 + 0.1 * jax.random.normal(key_list[16], (D,), jnp.float32), 0.5, 1.5),
        "up_weight": bell_draw(key_list[17], (D, FF), D ** -0.5, 0.25, ((0, 8), (1, 4))),
        "down_weight": bell_draw(key_list[18], (D, FF), FF ** -0.5, 0.125, ((0, 8), (1, 4))),
    }


EPS = 1e-05
HIGH = lax.Precision.HIGHEST

@jax.custom_vjp
def low(v):
    return lax.optimization_barrier(v.astype(jnp.bfloat16)).astype(jnp.float32)

@jax.custom_vjp
def low_back(v):
    return v

def low_keep(v):
    return (low(v), None)

def low_pass(kept, grad):
    return (grad,)

def back_keep(v):
    return (v, None)

def back_low(kept, grad):
    return (low(grad),)
low.defvjp(low_keep, low_pass)
low_back.defvjp(back_keep, back_low)

def matmul(left, right):
    return jnp.dot(left, right, precision=HIGH)

def normalize(values, gain_vec):
    return values * lax.rsqrt(lax.optimization_barrier(jnp.mean(values * values, axis=-1, keepdims=True)) + EPS) * gain_vec

def scan_block(state_in, portion, rates, skip):

    def advance(state_now, row_items):
        step_row, conv_row, b_row, c_row, keep_row = row_items
        state_now = jnp.exp(step_row[None, :] * rates) * keep_row * state_now + b_row[:, None] * (step_row * conv_row)[None, :]
        return (state_now, lax.optimization_barrier(jnp.sum(c_row[:, None] * state_now, axis=0)) + skip * conv_row)
    return lax.scan(advance, state_in, portion)

def selective(step_size, conv_x, b_rows, c_rows, keep_flag, rates, skip):
    blocks = LEN // SBLK

    def to_blocks(source):
        return source.reshape((blocks, SBLK) + source.shape[1:])
    checked = jax.checkpoint(scan_block)

    def run_block(state_in, portion):
        return checked(state_in, portion, rates, skip)
    initial = jnp.zeros(rates.shape, jnp.float32)
    final_state, outputs = lax.scan(run_block, initial, (to_blocks(step_size), to_blocks(conv_x), to_blocks(b_rows), to_blocks(c_rows), to_blocks(keep_flag)))
    return outputs.reshape(conv_x.shape)

def attention_rows(query_rows, key_rows, value_rows, seg_query, seg_keys, positions):
    scale = 1.0 / math.sqrt(HD)
    scores = low_back(jnp.einsum('qhd,khd->hqk', query_rows, key_rows, precision=HIGH) * scale)
    key_pos = jnp.arange(key_rows.shape[0]).astype(jnp.int32)
    allowed = (key_pos[None, :] <= positions[:, None]) & (seg_keys[None, :] == seg_query[:, None])
    scores = jnp.where(allowed[None], scores, -jnp.inf)
    row_peak = lax.optimization_barrier(jnp.max(scores, axis=-1, keepdims=True))
    weights_e = jnp.exp(scores - row_peak)
    probs_row = weights_e / lax.optimization_barrier(jnp.sum(weights_e, axis=-1, keepdims=True))
    return jnp.einsum('hqk,khd->qhd', low(probs_row), value_rows, precision=HIGH)

def layer(params, stream, segments):
    gain_one, in_w, conv_w, conv_b, xproj_w, dtproj_w, dt_b, alog, skip, out_w, gain_two, qkv_w, attn_w, gain_three, up_w, down_w = params
    row_count = stream.shape[0]
    mamba_in = low(normalize(stream, gain_one))
    projected = low_back(matmul(mamba_in, in_w.reshape(D, 2 * DI)))
    conv_input = projected[:, :DI]
    gate_input = projected[:, DI:]
    padded = jnp.concatenate([jnp.zeros((KC - 1, DI), jnp.float32), conv_input], 0)
    padded_ids = jnp.concatenate([jnp.full((KC - 1,), -1, jnp.int32), segments], 0)
    conv_pre = conv_b + jnp.zeros((row_count, DI), jnp.float32)
    for offset in range(KC):
        same_doc = (padded_ids[offset:offset + row_count] == segments).astype(jnp.float32)
        conv_pre = conv_pre + conv_w[offset] * padded[offset:offset + row_count] * same_doc[:, None]
    conv_x = low(jax.nn.silu(conv_pre))
    mixed = low(low_back(matmul(conv_x, xproj_w)))
    step_size = jax.nn.softplus(low_back(matmul(mixed[:, :RANK], dtproj_w)) + dt_b)
    keep_flag = jnp.concatenate([jnp.zeros((1,), jnp.float32), (segments[1:] == segments[:-1]).astype(jnp.float32)], 0)
    rates = -jnp.exp(alog).T
    scanned = selective(step_size, conv_x, mixed[:, RANK:RANK + NST], mixed[:, RANK + NST:], keep_flag, rates, skip)
    gated = low(scanned * jax.nn.silu(gate_input))
    after_mixer = stream + low_back(matmul(gated, out_w.T))
    attn_in = low(normalize(after_mixer, gain_two))
    qkv_rows = low(low_back(matmul(attn_in, qkv_w.reshape(D, 3 * H * HD)))).reshape(row_count, 3, H, HD)
    checked = jax.checkpoint(attention_rows)
    pieces = []
    for start_row in range(0, row_count, QBLK):
        end_row = start_row + QBLK
        positions = (start_row + jnp.arange(QBLK)).astype(jnp.int32)
        pieces.append(checked(qkv_rows[start_row:end_row, 0], qkv_rows[:end_row, 1], qkv_rows[:end_row, 2], segments[start_row:end_row], segments[:end_row], positions))
    attended = low(low_back(jnp.concatenate(pieces, 0).reshape(row_count, H * HD)))
    after_attn = after_mixer + low_back(matmul(attended, attn_w.T))
    ffn_in = low(normalize(after_attn, gain_three))
    hidden = low(jax.nn.gelu(low_back(matmul(ffn_in, up_w))))
    return after_attn + low_back(matmul(hidden, down_w.T))

def reference(tokens, segment_ids, out_grad, norm1_gain, in_weight, conv_weight, conv_bias, xproj_weight, dtproj_weight, dt_bias, a_log, d_skip, out_weight, norm2_gain, qkv_weight, attn_out_weight, norm3_gain, up_weight, down_weight):
    params = tuple((item.astype(jnp.float32) for item in (norm1_gain, in_weight, conv_weight, conv_bias, xproj_weight, dtproj_weight, dt_bias, a_log, d_skip, out_weight, norm2_gain, qkv_weight, attn_out_weight, norm3_gain, up_weight, down_weight)))
    seq_count = tokens.shape[0] // LEN
    streams = tokens.astype(jnp.float32).reshape(seq_count, LEN, D)
    cotangents = out_grad.astype(jnp.float32).reshape(seq_count, LEN, D)
    seq_ids = segment_ids.reshape(seq_count, LEN)

    def per_sequence(totals, packed):
        stream, cotangent, segments = packed

        def apply_layer(weights_all, stream_in):
            return layer(weights_all, stream_in, segments)
        output, pullback = jax.vjp(apply_layer, params, stream)
        weight_grads, stream_grad = pullback(cotangent)
        totals = jax.tree.map(jnp.add, totals, weight_grads)
        return (totals, (output, stream_grad))
    zero_grads = jax.tree.map(jnp.zeros_like, params)
    grads, (outputs, input_grads) = lax.scan(per_sequence, zero_grads, (streams, cotangents, seq_ids))
    gain_one, in_w, conv_w, conv_b, xproj_w, dtproj_w, dt_b, alog, skip, out_w, gain_two, qkv_w, attn_w, gain_three, up_w, down_w = grads
    return (outputs.reshape(-1, D).astype(jnp.bfloat16), input_grads.reshape(-1, D), gain_one, in_w, conv_w, conv_b, xproj_w, dtproj_w, dt_b, alog, skip, out_w, gain_two, qkv_w, attn_w, gain_three, up_w, down_w)
```

```python
import math

import jax
import jax.numpy as jnp
from jax import lax
from jax.experimental import pallas as pl
from jax.experimental.pallas import tpu as pltpu
from jax.sharding import PartitionSpec as P

NST = 16
RANK = 32
KC = 4
HD = 64
LEN = 1024
QBLK = 512
SBLK = 256


EPS = 1e-05
BIG = 1e30


def normalize(values, gain_vec):
    inverse = lax.rsqrt(jnp.mean(values * values, axis=-1, keepdims=True) + EPS)
    return (values * inverse * gain_vec, inverse)


def normalize_back(values, inverse, gain_vec, upstream):
    gain_grad = jnp.sum(upstream * values * inverse, axis=0)
    scaled = upstream * gain_vec
    inner_sum = jnp.mean(scaled * values, axis=-1, keepdims=True)
    return (inverse * scaled - values * inverse * inverse * inverse * inner_sum, gain_grad)


def silu_back(values, upstream):
    return jax.vjp(jax.nn.silu, values)[1](upstream)[0]


def gelu_back(values, upstream):
    return jax.vjp(jax.nn.gelu, values)[1](upstream)[0]


def spread(rows_low):
    return lax.all_gather(rows_low, "tp", axis=0, tiled=True)


def reduce_rows(left, right, pattern, local_rows):
    portion = lax.slice_in_dim(left, 0, lax.axis_size("tp") * local_rows, axis=0)
    return lax.psum_scatter(
        jnp.einsum(pattern, portion, right, preferred_element_type=jnp.float32),
        "tp",
        scatter_dimension=0,
        tiled=True,
    )


def channel_sum(partial_rows):
    return lax.psum(partial_rows, "tp")


def shift_down(source, amount):
    if amount == 0:
        return source
    return jnp.concatenate(
        [jnp.zeros((amount,) + source.shape[1:], source.dtype), source[:-amount]], 0
    )


def shift_up(source, amount):
    if amount == 0:
        return source
    return jnp.concatenate(
        [source[amount:], jnp.zeros((amount,) + source.shape[1:], source.dtype)], 0
    )


def conv_masks(segments, width):
    row_count = segments.shape[0]
    padded_ids = jnp.concatenate([jnp.full((width - 1,), -1, jnp.int32), segments], 0)
    return [
        (padded_ids[offset : offset + row_count] == segments).astype(jnp.float32)[:, None]
        for offset in range(width)
    ]


LOG2E = 1.4426950408889634
GT = 16
TB = 128

def softplus(v):
    return jnp.maximum(v, 0.0) + jnp.log1p(jnp.exp(-jnp.abs(v)))

def dot32(a, b, dims=((1,), (0,))):
    return lax.dot_general(a, b, (dims, ((), ())), preferred_element_type=jnp.float32)

def eye_rows(rows, cols, shift):
    r = lax.broadcasted_iota(jnp.int32, (rows, cols), 0)
    c = lax.broadcasted_iota(jnp.int32, (rows, cols), 1)
    return (c == r + shift).astype(jnp.bfloat16)

def spread_cols(rows_low):
    n = lax.broadcasted_iota(jnp.int32, (NST, GT * NST), 0)
    col = lax.broadcasted_iota(jnp.int32, (NST, GT * NST), 1)
    wide = dot32(rows_low, (col % NST == n).astype(jnp.bfloat16))
    t = lax.broadcasted_iota(jnp.int32, (TB, GT * NST), 0)
    col2 = lax.broadcasted_iota(jnp.int32, (TB, GT * NST), 1)
    return jnp.where(t % GT == col2 // NST, wide, 0.0).astype(jnp.bfloat16)

def fwd_kernel(conv_ref, mixed_ref, big_ref, gate_ref, dtproj_ref, dtb_ref, rates_ref, skip_ref,
               states_ref, scanned_ref, gated_ref, h_ref, step_ref, u_ref):
    C = conv_ref.shape[1]
    @pl.when(pl.program_id(0) == 0)
    def _():
        h_ref[...] = jnp.zeros_like(h_ref)
    conv = conv_ref[...].astype(jnp.float32)
    mixed = mixed_ref[...]
    step = softplus(dot32(mixed[:, :RANK], dtproj_ref[...]) + dtb_ref[...])
    step_ref[...] = jnp.maximum(step, big_ref[...])
    u_ref[...] = step * conv
    b_t = dot32(eye_rows(NST, RANK + 2 * NST, RANK), mixed, ((1,), (1,)))
    c_wide = spread_cols(mixed[:, RANK + NST:])
    rates = rates_ref[...]

    def group(g, h):
        bg = pltpu.roll(b_t, (TB - g * GT) % TB, axis=1)
        for j in range(GT):
            t = g * GT + j
            decay = jnp.exp2(step_ref[pl.ds(t, 1), :] * rates)
            drive = u_ref[pl.ds(t, 1), :] * bg[:, j:j + 1]
            h = decay * h + drive
            states_ref[pl.ds(pl.multiple_of(t * NST, NST), NST), :] = h.astype(jnp.bfloat16)
        return h
    h_ref[...] = lax.fori_loop(0, TB // GT, group, h_ref[...])
    skip = skip_ref[...]
    for g in range(TB // GT):
        rows = slice(g * GT, (g + 1) * GT)
        y = dot32(c_wide[rows], states_ref[g * GT * NST:(g + 1) * GT * NST, :])
        y = y + skip * conv[rows]
        scanned_ref[rows, :] = y
        gate = gate_ref[rows, :]
        gated_ref[rows, :] = (y * (gate * jax.nn.sigmoid(gate))).astype(jnp.bfloat16)

def bwd_kernel(conv_ref, mixed_ref, big_ref, gate_ref, scanned_ref, gg_ref, dtproj_ref, dtb_ref, rates_ref, skip_ref,
               states_ref, prev_ref,
               gate_grad_ref, step_low_ref, conv_grad_ref, mixed_grad_ref, dtb_grad_ref, rate_grad_ref, skip_grad_ref,
               e_ref, step_ref, u_ref, dy_ref, g_ref, w_ref):
    C = conv_ref.shape[1]
    @pl.when(pl.program_id(0) == 0)
    def _():
        e_ref[...] = jnp.zeros_like(e_ref)
        dtb_grad_ref[...] = jnp.zeros_like(dtb_grad_ref)
        rate_grad_ref[...] = jnp.zeros_like(rate_grad_ref)
        skip_grad_ref[...] = jnp.zeros_like(skip_grad_ref)
    conv = conv_ref[...].astype(jnp.float32)
    mixed = mixed_ref[...]
    step_in = dot32(mixed[:, :RANK], dtproj_ref[...]) + dtb_ref[...]
    step = softplus(step_in)
    step_ref[...] = jnp.maximum(step, big_ref[...])
    u = step * conv
    gate = gate_ref[...]
    sig = jax.nn.sigmoid(gate)
    gg = gg_ref[...]
    dy = gg * (gate * sig)
    gate_grad_ref[...] = (gg * scanned_ref[...] * (sig + gate * sig * (1.0 - sig))).astype(jnp.bfloat16)
    dy_ref[...] = dy
    skip_grad_ref[...] += jnp.sum(dy * conv, axis=0, keepdims=True)
    c_t = dot32(eye_rows(NST, RANK + 2 * NST, RANK + NST), mixed, ((1,), (1,)))
    b_wide = spread_cols(mixed[:, RANK:RANK + NST])
    rates = rates_ref[...]

    def one(t, j, cg, e, acc, h_prev):
        step_row = step_ref[pl.ds(t, 1), :]
        decay = jnp.exp2(step_row * rates)
        G = cg[:, j:j + 1] * dy_ref[pl.ds(t, 1), :] + e
        e = decay * G
        W = e * h_prev
        acc = acc + W * step_row
        at = pl.ds(pl.multiple_of(t * NST, NST), NST)
        g_ref[at, :] = G.astype(jnp.bfloat16)
        w_ref[at, :] = (W * rates).astype(jnp.bfloat16)
        return e, acc

    def group(i, carry):
        e, acc = carry
        g = TB // GT - 1 - i
        cg = pltpu.roll(c_t, (TB - g * GT) % TB, axis=1)
        for j in range(GT - 1, -1, -1):
            t = g * GT + j
            if j > 0:
                h_prev = states_ref[pl.ds(pl.multiple_of((t - 1) * NST, NST), NST), :].astype(jnp.float32)
            else:
                at = jnp.maximum(t - 1, 0) * NST
                inner = states_ref[pl.ds(pl.multiple_of(at, NST), NST), :].astype(jnp.float32)
                h_prev = jnp.where(g == 0, prev_ref[...].astype(jnp.float32), inner)
            e, acc = one(t, j, cg, e, acc, h_prev)
        return e, acc
    e, acc = lax.fori_loop(0, TB // GT, group, (e_ref[...], jnp.zeros((NST, C), jnp.float32)))
    e_ref[...] = e
    rate_grad_ref[...] += acc
    skip = skip_ref[...]
    u_low = u.astype(jnp.bfloat16)
    dy_low = dy.astype(jnp.bfloat16)
    ones_wide = spread_cols(jnp.ones((TB, NST), jnp.bfloat16))
    lane = lax.broadcasted_iota(jnp.int32, (NST, TB), 1)
    bg_t = jnp.zeros((NST, TB), jnp.float32)
    cg_t = jnp.zeros((NST, TB), jnp.float32)
    for g in range(TB // GT):
        rows = slice(g * GT, (g + 1) * GT)
        wide = slice(g * GT * NST, (g + 1) * GT * NST)
        G = g_ref[wide, :]
        along_b = dot32(b_wide[rows], G)
        sg = dot32(ones_wide[rows], w_ref[wide, :]) * (1.0 / LOG2E) + along_b * conv[rows]
        conv_grad_ref[rows, :] = along_b * step[rows] + skip * dy[rows]
        sig_in = sg * jax.nn.sigmoid(step_in[rows])
        dtb_grad_ref[...] += jnp.sum(sig_in, axis=0, keepdims=True)
        step_low_ref[rows, :] = sig_in.astype(jnp.bfloat16)
        mb = dot32(G, u_low, ((1,), (1,)))
        mc = dot32(states_ref[wide, :], dy_low, ((1,), (1,)))
        for j in range(GT):
            t = g * GT + j
            bg_t = jnp.where(lane == t, mb[j * NST:(j + 1) * NST], bg_t)
            cg_t = jnp.where(lane == t, mc[j * NST:(j + 1) * NST], cg_t)
    rank_part = dot32(step_low_ref[...], dtproj_ref[...], ((1,), (1,)))
    bc = jnp.concatenate([bg_t, cg_t], axis=0)
    mixed_grad_ref[...] = jnp.concatenate([rank_part, bc.T], axis=1)

def scan_fwd(conv_low, mixed_low, big, gate, dtproj, dtb, rates2, skip):
    T, C = conv_low.shape
    nb = T // TB
    row = lambda w: pl.BlockSpec((TB, w), lambda i: (i, 0))
    whole = lambda a: pl.BlockSpec(a.shape, lambda i: (0, 0))
    return pl.pallas_call(
        fwd_kernel,
        grid=(nb,),
        in_specs=[row(C), row(64), row(1), row(C), whole(dtproj), whole(dtb), whole(rates2), whole(skip)],
        out_specs=[pl.BlockSpec((TB * NST, C), lambda i: (i, 0)), row(C), row(C)],
        out_shape=[jax.ShapeDtypeStruct((T * NST, C), jnp.bfloat16), jax.ShapeDtypeStruct((T, C), jnp.float32), jax.ShapeDtypeStruct((T, C), jnp.bfloat16)],
        scratch_shapes=[pltpu.VMEM((NST, C), jnp.float32), pltpu.VMEM((TB, C), jnp.float32), pltpu.VMEM((TB, C), jnp.float32)],
        compiler_params=pltpu.CompilerParams(dimension_semantics=("arbitrary",)),
        name="scan_forward",
    )(conv_low, mixed_low, big, gate, dtproj, dtb, rates2, skip)

def scan_bwd(conv_low, mixed_low, big, gate, scanned, gated_grad, dtproj, dtb, rates2, skip, states):
    T, C = conv_low.shape
    nb = T // TB
    row = lambda w: pl.BlockSpec((TB, w), lambda i: (nb - 1 - i, 0))
    whole = lambda a: pl.BlockSpec(a.shape, lambda i: (0, 0))
    fixed = lambda r, c: pl.BlockSpec((r, c), lambda i: (0, 0))
    f32 = lambda s: jax.ShapeDtypeStruct(s, jnp.float32)
    low = lambda s: jax.ShapeDtypeStruct(s, jnp.bfloat16)
    return pl.pallas_call(
        bwd_kernel,
        grid=(nb,),
        in_specs=[row(C), row(64), row(1), row(C), row(C), row(C), whole(dtproj), whole(dtb), whole(rates2), whole(skip),
                  pl.BlockSpec((TB * NST, C), lambda i: (nb - 1 - i, 0)),
                  pl.BlockSpec((NST, C), lambda i: (jnp.maximum((nb - 1 - i) * TB - 1, 0), 0))],
        out_specs=[row(C), row(C), row(C), row(64), fixed(1, C), fixed(NST, C), fixed(1, C)],
        out_shape=[low((T, C)), low((T, C)), f32((T, C)), f32((T, 64)), f32((1, C)), f32((NST, C)), f32((1, C))],
        scratch_shapes=[pltpu.VMEM((NST, C), jnp.float32), pltpu.VMEM((TB, C), jnp.float32), pltpu.VMEM((TB, C), jnp.float32), pltpu.VMEM((TB, C), jnp.float32),
                        pltpu.VMEM((TB * NST, C), jnp.bfloat16), pltpu.VMEM((TB * NST, C), jnp.bfloat16)],
        compiler_params=pltpu.CompilerParams(dimension_semantics=("arbitrary",)),
        name="scan_backward",
    )(conv_low, mixed_low, big, gate, scanned, gated_grad, dtproj, dtb, rates2, skip, states, states)


def block_scores(query_rows, key_rows, seg_query, seg_keys, start_row):
    scores = jnp.einsum(
        "qhd,khd->hqk", query_rows, key_rows, preferred_element_type=jnp.float32
    ) * (1.0 / math.sqrt(HD))
    shape_qk = (query_rows.shape[0], key_rows.shape[0])
    key_pos = lax.broadcasted_iota(jnp.int32, shape_qk, 1)
    query_pos = lax.broadcasted_iota(jnp.int32, shape_qk, 0) + start_row
    allowed = (key_pos <= query_pos) & (seg_keys[None, :] == seg_query[:, None])
    return jnp.where(allowed[None], scores, -jnp.inf)


def attend_sequence(query_rows, key_rows, value_rows, segments):
    outputs = []
    totals = []
    for start_row in range(0, LEN, QBLK):
        end_row = start_row + QBLK
        scores = block_scores(
            query_rows[start_row:end_row],
            key_rows[:end_row],
            segments[start_row:end_row],
            segments[:end_row],
            start_row,
        )
        row_peak = jnp.max(scores, axis=-1, keepdims=True)
        log_total = row_peak + jnp.log(jnp.sum(jnp.exp(scores - row_peak), axis=-1, keepdims=True))
        probs_low = jnp.exp(scores - log_total).astype(jnp.bfloat16)
        outputs.append(
            jnp.einsum(
                "hqk,khd->qhd", probs_low, value_rows[:end_row], preferred_element_type=jnp.float32
            )
        )
        totals.append(log_total)
    return (jnp.concatenate(outputs, 0), jnp.stack(totals, 0))


def attend_back(query_rows, key_rows, value_rows, segments, totals, grad_rows):
    scale = 1.0 / math.sqrt(HD)
    query_grads = []
    key_grad = jnp.zeros(key_rows.shape, jnp.float32)
    value_grad = jnp.zeros(value_rows.shape, jnp.float32)
    for number, start_row in enumerate(range(0, LEN, QBLK)):
        end_row = start_row + QBLK
        scores = block_scores(
            query_rows[start_row:end_row],
            key_rows[:end_row],
            segments[start_row:end_row],
            segments[:end_row],
            start_row,
        )
        probs_full = jnp.exp(scores - totals[number])
        probs_low = probs_full.astype(jnp.bfloat16)
        grad_block = grad_rows[start_row:end_row]
        prob_grad = jnp.einsum(
            "qhd,khd->hqk", grad_block, value_rows[:end_row], preferred_element_type=jnp.float32
        )
        inner_sum = jnp.sum(probs_full * prob_grad, axis=-1, keepdims=True)
        score_grad = (probs_full * (prob_grad - inner_sum)).astype(jnp.bfloat16)
        query_grads.append(
            jnp.einsum(
                "hqk,khd->qhd", score_grad, key_rows[:end_row], preferred_element_type=jnp.float32
            )
            * scale
        )
        key_grad = key_grad.at[:end_row].add(
            jnp.einsum(
                "hqk,qhd->khd",
                score_grad,
                query_rows[start_row:end_row],
                preferred_element_type=jnp.float32,
            )
            * scale
        )
        value_grad = value_grad.at[:end_row].add(
            jnp.einsum("hqk,qhd->khd", probs_low, grad_block, preferred_element_type=jnp.float32)
        )
    return (jnp.concatenate(query_grads, 0), key_grad, value_grad)


def body(
    tokens,
    segment_ids,
    out_grad,
    norm1_gain,
    in_weight,
    conv_weight,
    conv_bias,
    xproj_weight,
    dtproj_weight,
    dt_bias,
    a_log,
    d_skip,
    out_weight,
    norm2_gain,
    qkv_weight,
    attn_out_weight,
    norm3_gain,
    up_weight,
    down_weight,
):
    local_rows = tokens.shape[0]
    stream = tokens.astype(jnp.float32)
    in_full, out_full, qkv_full, attn_full, up_full, down_full = (
        lax.all_gather(in_weight, "dp", axis=0, tiled=True),
        lax.all_gather(out_weight, "dp", axis=0, tiled=True),
        lax.all_gather(qkv_weight, "dp", axis=0, tiled=True),
        lax.all_gather(attn_out_weight, "dp", axis=0, tiled=True),
        lax.all_gather(up_weight, "dp", axis=0, tiled=True),
        lax.all_gather(down_weight, "dp", axis=0, tiled=True),
    )
    conv_taps, conv_offset, xproj_all, dtproj_all, dtbias_all, alog_all, skip_all = (
        conv_weight,
        conv_bias,
        xproj_weight,
        dtproj_weight,
        dt_bias,
        a_log,
        d_skip,
    )
    group_rows = segment_ids.shape[0]
    mamba_normed, mamba_inverse = normalize(stream, norm1_gain)
    mamba_rows = spread(mamba_normed.astype(jnp.bfloat16))
    projected = jnp.einsum("td,dkc->tkc", mamba_rows, in_full, preferred_element_type=jnp.float32)
    conv_input = projected[:, 0]
    gate_input = projected[:, 1]
    masks_all = conv_masks(segment_ids, KC)
    shifted = [shift_down(conv_input, KC - 1 - offset) * masks_all[offset] for offset in range(KC)]
    conv_pre = conv_offset + conv_taps[0] * shifted[0]
    for offset in range(1, KC):
        conv_pre = conv_pre + conv_taps[offset] * shifted[offset]
    conv_low = jax.nn.silu(conv_pre).astype(jnp.bfloat16)
    mixed_low = channel_sum(
        jnp.dot(conv_low, xproj_all, preferred_element_type=jnp.float32)
    ).astype(jnp.bfloat16)
    rank_rows = mixed_low[:, :RANK]
    rates = -jnp.exp(alog_all).T
    big = jnp.concatenate(
        [jnp.full((1,), BIG, jnp.float32), jnp.where(segment_ids[1:] == segment_ids[:-1], 0.0, BIG)], 0
    )[:, None]
    states, scanned, gated_low = scan_fwd(
        conv_low, mixed_low, big, gate_input, dtproj_all, dtbias_all[None], rates * LOG2E, skip_all[None]
    )
    after_mixer = stream + reduce_rows(gated_low, out_full, "tc,dc->td", local_rows)
    attn_normed, attn_inverse = normalize(after_mixer, norm2_gain)
    attn_rows = spread(attn_normed.astype(jnp.bfloat16))
    qkv_low = jnp.einsum(
        "td,dkc->tkc", attn_rows, qkv_full, preferred_element_type=jnp.float32
    ).astype(jnp.bfloat16)
    heads_local = qkv_low.shape[2] // HD
    seq_count = group_rows // LEN
    qkv_split = qkv_low.reshape(seq_count, LEN, 3, heads_local, HD)
    seq_segments = segment_ids.reshape(seq_count, LEN)

    def forward_sequence(packed):
        qkv_seq, seq_ids = packed
        return attend_sequence(qkv_seq[:, 0], qkv_seq[:, 1], qkv_seq[:, 2], seq_ids)

    attended, totals = lax.map(forward_sequence, (qkv_split, seq_segments))
    attended_low = attended.reshape(group_rows, heads_local * HD).astype(jnp.bfloat16)
    after_attn = after_mixer + reduce_rows(attended_low, attn_full, "tc,dc->td", local_rows)
    ffn_normed, ffn_inverse = normalize(after_attn, norm3_gain)
    top_grad = out_grad.astype(jnp.float32)
    ffn_rows = spread(ffn_normed.astype(jnp.bfloat16))
    hidden_in = jnp.dot(ffn_rows, up_full, preferred_element_type=jnp.float32)
    hidden_low = jax.nn.gelu(hidden_in).astype(jnp.bfloat16)
    feed = reduce_rows(hidden_low, down_full, "tf,df->td", local_rows)
    result = (after_attn + feed).astype(jnp.bfloat16)
    feed_rows = spread(out_grad)
    hidden_grad = jnp.dot(feed_rows, down_full, preferred_element_type=jnp.float32)
    down_grad = jnp.einsum("td,tf->df", feed_rows, hidden_low, preferred_element_type=jnp.float32)
    up_in_grad = gelu_back(hidden_in, hidden_grad).astype(jnp.bfloat16)
    up_grad = jnp.einsum("td,tf->df", ffn_rows, up_in_grad, preferred_element_type=jnp.float32)
    ffn_grad = reduce_rows(up_in_grad, up_full, "tf,df->td", local_rows)
    ffn_input_grad, gain_three_grad = normalize_back(after_attn, ffn_inverse, norm3_gain, ffn_grad)
    attn_stream_grad = top_grad + ffn_input_grad
    attn_branch_rows = spread(attn_stream_grad.astype(jnp.bfloat16))
    attended_grad = jnp.dot(attn_branch_rows, attn_full, preferred_element_type=jnp.float32).astype(
        jnp.bfloat16
    )
    attn_weight_grad = jnp.einsum(
        "td,tc->dc", attn_branch_rows, attended_low, preferred_element_type=jnp.float32
    )
    grad_split = attended_grad.reshape(seq_count, LEN, heads_local, HD)

    def backward_sequence(packed):
        qkv_seq, seq_ids, seq_totals, seq_grad = packed
        return attend_back(
            qkv_seq[:, 0], qkv_seq[:, 1], qkv_seq[:, 2], seq_ids, seq_totals, seq_grad
        )

    query_grad, key_grad, value_grad = lax.map(
        backward_sequence, (qkv_split, seq_segments, totals, grad_split)
    )
    qkv_grad_low = (
        jnp.stack([query_grad, key_grad, value_grad], 2)
        .reshape(group_rows, 3, heads_local * HD)
        .astype(jnp.bfloat16)
    )
    qkv_weight_grad = jnp.einsum(
        "td,tkc->dkc", attn_rows, qkv_grad_low, preferred_element_type=jnp.float32
    )
    attn_in_grad = reduce_rows(qkv_grad_low, qkv_full, "tkc,dkc->td", local_rows)
    attn_input_grad, gain_two_grad = normalize_back(
        after_mixer, attn_inverse, norm2_gain, attn_in_grad
    )
    mixer_stream_grad = attn_stream_grad + attn_input_grad
    mixer_branch_rows = spread(mixer_stream_grad.astype(jnp.bfloat16))
    gated_grad = jnp.dot(mixer_branch_rows, out_full, preferred_element_type=jnp.float32)
    out_weight_grad = jnp.einsum(
        "td,tc->dc", mixer_branch_rows, gated_low, preferred_element_type=jnp.float32
    )
    gate_grad, step_low, conv_scan_grad, mixed_part, dt_bias_grad, rate_grad, skip_grad = scan_bwd(
        conv_low, mixed_low, big, gate_input, scanned, gated_grad,
        dtproj_all, dtbias_all[None], rates * LOG2E, skip_all[None], states,
    )
    dt_bias_grad = dt_bias_grad[0]
    skip_grad = skip_grad[0]
    dtproj_grad = jnp.einsum("tr,tc->rc", rank_rows, step_low, preferred_element_type=jnp.float32)
    mixed_grad = channel_sum(mixed_part).astype(jnp.bfloat16)
    xproj_grad = jnp.einsum("tc,tk->ck", conv_low, mixed_grad, preferred_element_type=jnp.float32)
    conv_grad = conv_scan_grad + jnp.einsum(
        "tk,ck->tc", mixed_grad, xproj_all, preferred_element_type=jnp.float32
    )
    pre_grad = silu_back(conv_pre, conv_grad)
    conv_bias_grad = jnp.sum(pre_grad, axis=0)
    conv_weight_grad = jnp.stack(
        [jnp.sum(pre_grad * shifted[offset], axis=0) for offset in range(KC)], 0
    )
    conv_input_grad = shift_up(pre_grad * masks_all[0] * conv_taps[0], KC - 1)
    for offset in range(1, KC):
        conv_input_grad = conv_input_grad + shift_up(
            pre_grad * masks_all[offset] * conv_taps[offset], KC - 1 - offset
        )
    proj_grad_low = jnp.stack([conv_input_grad.astype(jnp.bfloat16), gate_grad], 1)
    in_weight_grad = jnp.einsum(
        "td,tkc->dkc", mamba_rows, proj_grad_low, preferred_element_type=jnp.float32
    )
    mamba_in_grad = reduce_rows(proj_grad_low, in_full, "tkc,dkc->td", local_rows)
    mamba_input_grad, gain_one_grad = normalize_back(
        stream, mamba_inverse, norm1_gain, mamba_in_grad
    )
    input_grad = mixer_stream_grad + mamba_input_grad
    in_sum, out_sum, qkv_sum, attn_sum, up_sum, down_sum = (
        lax.psum_scatter(
            in_weight_grad.astype(jnp.bfloat16), "dp", scatter_dimension=0, tiled=True
        ).astype(jnp.float32),
        lax.psum_scatter(
            out_weight_grad.astype(jnp.bfloat16), "dp", scatter_dimension=0, tiled=True
        ).astype(jnp.float32),
        lax.psum_scatter(
            qkv_weight_grad.astype(jnp.bfloat16), "dp", scatter_dimension=0, tiled=True
        ).astype(jnp.float32),
        lax.psum_scatter(
            attn_weight_grad.astype(jnp.bfloat16), "dp", scatter_dimension=0, tiled=True
        ).astype(jnp.float32),
        lax.psum_scatter(
            up_grad.astype(jnp.bfloat16), "dp", scatter_dimension=0, tiled=True
        ).astype(jnp.float32),
        lax.psum_scatter(
            down_grad.astype(jnp.bfloat16), "dp", scatter_dimension=0, tiled=True
        ).astype(jnp.float32),
    )
    convw_sum, convb_sum, xproj_sum, dtproj_sum, dtbias_sum, rate_total, skip_total = (
        lax.psum(conv_weight_grad.astype(jnp.bfloat16), "dp").astype(jnp.float32),
        lax.psum(conv_bias_grad.astype(jnp.bfloat16), "dp").astype(jnp.float32),
        lax.psum(xproj_grad.astype(jnp.bfloat16), "dp").astype(jnp.float32),
        lax.psum(dtproj_grad.astype(jnp.bfloat16), "dp").astype(jnp.float32),
        lax.psum(dt_bias_grad.astype(jnp.bfloat16), "dp").astype(jnp.float32),
        lax.psum(rate_grad.astype(jnp.bfloat16), "dp").astype(jnp.float32),
        lax.psum(skip_grad.astype(jnp.bfloat16), "dp").astype(jnp.float32),
    )
    gain_one_sum, gain_two_sum, gain_three_sum = lax.psum(
        (gain_one_grad, gain_two_grad, gain_three_grad), ("dp", "tp")
    )
    local_rates = -jnp.exp(a_log).T
    alog_grad = (rate_total * local_rates).T
    return (
        result,
        input_grad,
        gain_one_sum,
        in_sum,
        convw_sum,
        convb_sum,
        xproj_sum,
        dtproj_sum,
        dtbias_sum,
        alog_grad,
        skip_total,
        out_sum,
        gain_two_sum,
        qkv_sum,
        attn_sum,
        gain_three_sum,
        up_sum,
        down_sum,
    )


def solution(mesh):
    return jax.shard_map(
        body,
        mesh=mesh,
        in_specs=(
            P(("dp", "tp"), None),
            P("dp"),
            P(("dp", "tp"), None),
            P(),
            P("dp", None, "tp"),
            P(None, "tp"),
            P("tp"),
            P("tp", None),
            P(None, "tp"),
            P("tp"),
            P("tp", None),
            P("tp"),
            P("dp", "tp"),
            P(),
            P("dp", None, "tp"),
            P("dp", "tp"),
            P(),
            P("dp", "tp"),
            P("dp", "tp"),
        ),
        out_specs=(
            P(("dp", "tp"), None),
            P(("dp", "tp"), None),
            P(),
            P("dp", None, "tp"),
            P(None, "tp"),
            P("tp"),
            P("tp", None),
            P(None, "tp"),
            P("tp"),
            P("tp", None),
            P("tp"),
            P("dp", "tp"),
            P(),
            P("dp", None, "tp"),
            P("dp", "tp"),
            P(),
            P("dp", "tp"),
            P("dp", "tp"),
        ),
        check_vma=False,
    )
```

```python
import functools
import math

import jax
import jax.numpy as jnp
from jax import lax
from jax.experimental import pallas as pl
from jax.experimental.pallas import tpu as pltpu
from jax.sharding import PartitionSpec as P

NST = 16
RANK = 32
MIX = RANK + 2 * NST
KC = 4
HD = 64
LEN = 1024
QBLK = 512
GT = 16
TB = 128
PARTS = 2
OUTER = 4
EPS = 1e-05
BIG = 1e30
LOG2E = 1.4426950408889634
MESH = pl.DeviceIdType.MESH
VM = pl.BlockSpec(memory_space=pltpu.VMEM)
ANY = pl.BlockSpec(memory_space=pl.ANY)
F32 = jnp.float32
BF16 = jnp.bfloat16


def shaped(shape, dtype):
    return jax.ShapeDtypeStruct(shape, dtype)


def dma(count):
    return pltpu.SemaphoreType.DMA((count,))


def rows_of(index, count):
    return pl.ds(pl.multiple_of(index * count, count), count)


def remote(src, dst, send_sem, recv_sem, axis, device):
    return pltpu.make_async_remote_copy(
        src_ref=src, dst_ref=dst, send_sem=send_sem, recv_sem=recv_sem,
        device_id={axis: device}, device_id_type=MESH,
    )


class Place:
    def __init__(self, tp, dp):
        self.tp, self.dp, self.chips = tp, dp, tp // 2
        self.me = lax.axis_index("tp")
        self.y, self.c = lax.div(self.me, 2), lax.rem(self.me, 2)
        self.d = lax.axis_index("dp")
        self.inner_size = dp // OUTER
        self.do, self.di = lax.div(self.d, self.inner_size), lax.rem(self.d, self.inner_size)
        self.sibling = self.y * 2 + 1 - self.c

    def chip(self, k):
        return lax.rem(self.y + k, self.chips)

    def peer(self, k):
        return self.chip(k) * 2 + self.c

    def along(self, k):
        return lax.rem(self.d + k, self.dp)

    def outer_of(self, k):
        return lax.rem(self.do + k, OUTER)

    def inner_of(self, m):
        return lax.rem(self.di + m, self.inner_size)

    def outer(self, k):
        return self.outer_of(k) * self.inner_size + self.di

    def inner(self, m):
        return self.do * self.inner_size + self.inner_of(m)

    def barrier(self, whole_dp=False):
        sem = pltpu.get_barrier_semaphore()
        pl.semaphore_signal(sem, inc=1, device_id={"tp": self.sibling}, device_id_type=MESH)
        for k in range(1, self.chips):
            pl.semaphore_signal(sem, inc=1, device_id={"tp": self.peer(k)}, device_id_type=MESH)
        others = [self.outer(k) for k in range(1, OUTER)] + [self.inner(m) for m in range(1, self.inner_size)]
        if whole_dp:
            others = [self.along(k) for k in range(1, self.dp)]
        for other in others:
            pl.semaphore_signal(sem, inc=1, device_id={"dp": other}, device_id_type=MESH)
        count = self.chips + len(others)
        pl.semaphore_wait(sem, count)


def tp_rows(place, k, core, count, s, parts):
    size = count // parts
    return pl.ds(pl.multiple_of((place.chip(k) * 2 + core) * count + s * size, size), size)


class TpScatter:
    @staticmethod
    def scratch(tp, rows, width):
        count = tp // 2 * PARTS
        return [pltpu.VMEM((count, rows // PARTS, width), BF16)] * 3 + [dma(count)] * 4

    def __init__(self, place, part, refs, value=None):
        self.p, self.part, self.value = place, part, value
        self.sib, self.mid_sum, self.got, self.s1, self.r1, self.s2, self.r2 = refs
        self.rows = self.sib.shape[1] * PARTS

    def first(self, k, s):
        p, n = self.p, k * PARTS + s
        src = self.part.at[tp_rows(p, k, 1 - p.c, self.rows, s, PARTS)]
        return remote(src, self.sib.at[n], self.s1.at[n], self.r1.at[n], "tp", p.sibling)

    def second(self, k, s):
        n = k * PARTS + s
        return remote(self.mid_sum.at[n], self.got.at[n], self.s2.at[n], self.r2.at[n], "tp", self.p.peer(k))

    def pair_sum(self, k, s):
        rows = tp_rows(self.p, k, self.p.c, self.rows, s, PARTS)
        mine = self.part[rows, :].astype(F32) if self.value is None else self.value(rows)
        return mine + self.sib[k * PARTS + s].astype(F32)

    def begin(self):
        for k in list(range(1, self.p.chips)) + [0]:
            for s in range(PARTS):
                if self.value is not None:
                    rows = tp_rows(self.p, k, 1 - self.p.c, self.rows, s, PARTS)
                    self.part[rows, :] = self.value(rows).astype(BF16)
                self.first(k, s).start()

    def mid(self):
        for s in range(PARTS):
            for k in range(1, self.p.chips):
                self.first(k, s).wait_recv()
                self.mid_sum[k * PARTS + s] = self.pair_sum(k, s).astype(BF16)
                self.second(k, s).start()

    def end(self, s):
        self.first(0, s).wait_recv()
        total = self.pair_sum(0, s)
        for k in range(1, self.p.chips):
            self.second(k, s).wait_recv()
            total = total + self.got[k * PARTS + s].astype(F32)
        return total

    def piece(self, s):
        size = self.rows // PARTS
        return pl.ds(s * size, size)

    def drain(self):
        for s in range(PARTS):
            for k in range(self.p.chips):
                self.first(k, s).wait_send()
            for k in range(1, self.p.chips):
                self.second(k, s).wait_send()


class TpGather:
    @staticmethod
    def scratch(tp):
        return [dma(tp // 2 * PARTS)] * 6

    def __init__(self, place, src, full, refs):
        self.p, self.src, self.full = place, src, full
        self.s1, self.r1, self.s2, self.r2, self.s3, self.r3 = refs
        self.rows = full.shape[0] // place.tp

    def own(self, s):
        size = self.rows // PARTS
        return self.full.at[pl.ds(pl.multiple_of(self.p.me * self.rows + s * size, size), size)]

    def mine(self, s):
        size = self.rows // PARTS
        return self.src.at[pl.ds(s * size, size)]

    def out(self, k, s):
        n = k * PARTS + s
        return remote(self.mine(s), self.own(s), self.s1.at[n], self.r1.at[n], "tp", self.p.peer(k))

    def side(self, s):
        return remote(self.mine(s), self.own(s), self.s2.at[s], self.r2.at[s], "tp", self.p.sibling)

    def onward(self, k, s):
        p, n = self.p, k * PARTS + s
        at = self.full.at[tp_rows(p, p.chips - k, p.c, self.rows, s, PARTS)]
        return remote(at, at, self.s3.at[n], self.r3.at[n], "tp", p.sibling)

    def begin(self, s):
        for k in range(1, self.p.chips):
            self.out(k, s).start()
        self.side(s).start()

    def mid(self):
        for s in range(PARTS):
            for k in range(1, self.p.chips):
                self.out(k, s).wait_recv()
                self.onward(k, s).start()

    def side_here(self):
        for s in range(PARTS):
            self.side(s).wait_recv()

    def onward_here(self, k):
        for s in range(PARTS):
            self.onward(k, s).wait_recv()

    def end(self):
        self.side_here()
        for k in range(1, self.p.chips):
            self.onward_here(k)

    def each(self, work, forward=True):
        p = self.p
        work(rows_of(p.me, self.rows))
        self.side_here()
        work(rows_of(p.sibling, self.rows))
        if forward:
            self.mid()
        for k in range(1, p.chips):
            work(rows_of(p.chip(p.chips - k) * 2 + p.c, self.rows))
        for k in range(1, p.chips):
            self.onward_here(k)
            work(rows_of(p.chip(p.chips - k) * 2 + 1 - p.c, self.rows))

    def drain(self):
        for s in range(PARTS):
            self.side(s).wait_send()
            for k in range(1, self.p.chips):
                self.out(k, s).wait_send()
                self.onward(k, s).wait_send()


class TpTotal:
    @staticmethod
    def scratch(tp, rows, width):
        chips = tp // 2
        return [pltpu.VMEM((rows, width), BF16)] * 2 + [pltpu.VMEM((chips, rows, width), BF16), dma(1), dma(1), dma(chips), dma(chips)]

    def __init__(self, place, part, refs):
        self.p, self.part = place, part
        self.sib, self.pair, self.got, self.s1, self.r1, self.s2, self.r2 = refs

    def first(self):
        return remote(self.part, self.sib, self.s1.at[0], self.r1.at[0], "tp", self.p.sibling)

    def second(self, k):
        return remote(self.pair, self.got.at[k], self.s2.at[k], self.r2.at[k], "tp", self.p.peer(k))

    def begin(self):
        self.first().start()

    def run(self):
        self.first().wait_recv()
        self.pair[...] = (self.part[...].astype(F32) + self.sib[...].astype(F32)).astype(BF16)
        for k in range(1, self.p.chips):
            self.second(k).start()
        total = self.pair[...].astype(F32)
        for k in range(1, self.p.chips):
            self.second(k).wait_recv()
            total = total + self.got[k].astype(F32)
        return total

    def drain(self):
        self.first().wait_send()
        for k in range(1, self.p.chips):
            self.second(k).wait_send()


class DpGather:
    @staticmethod
    def scratch(dp):
        return [dma(OUTER)] * 2 + [dma(dp)] * 2 + [dma(1)]

    def __init__(self, place, src, full, refs):
        self.p, self.src, self.full = place, src, full
        self.s1, self.r1, self.s2, self.r2, self.ls = refs
        self.rows = src.shape[0]

    def far(self, k):
        own = self.full.at[rows_of(self.p.d, self.rows)]
        return remote(self.src, own, self.s1.at[k], self.r1.at[k], "dp", self.p.outer(k))

    def near(self, k, m):
        p, n = self.p, k * self.p.inner_size + m
        at = self.full.at[rows_of(p.outer(OUTER - k), self.rows)]
        return remote(self.src if k == 0 else at, at, self.s2.at[n], self.r2.at[n], "dp", p.inner(m))

    def local(self):
        return pltpu.make_async_copy(self.src, self.full.at[rows_of(self.p.d, self.rows)], self.ls.at[0])

    def begin(self):
        for k in range(1, OUTER):
            self.far(k).start()
        for m in range(1, self.p.inner_size):
            self.near(0, m).start()
        self.local().start()

    def mid(self):
        for k in range(1, OUTER):
            self.far(k).wait_recv()
            for m in range(1, self.p.inner_size):
                self.near(k, m).start()

    def end(self):
        self.local().wait()
        for k in range(OUTER):
            for m in range(1, self.p.inner_size):
                self.near(k, m).wait_recv()

    def drain(self):
        for k in range(OUTER):
            if k:
                self.far(k).wait_send()
            for m in range(1, self.p.inner_size):
                self.near(k, m).wait_send()


class DpScatter:
    @staticmethod
    def scratch(dp, rows, width):
        block = pltpu.VMEM((OUTER, rows, width), BF16)
        return [block, pltpu.VMEM((dp, rows, width), BF16), block, block, dma(OUTER), dma(dp), dma(dp), dma(OUTER), dma(OUTER)]

    def __init__(self, place, part, refs):
        self.p, self.part = place, part
        self.own, self.near_got, self.mid_sum, self.far_got, self.ls, self.s1, self.r1, self.s2, self.r2 = refs
        self.rows = self.own.shape[1]

    def local(self, k):
        src = self.part.at[rows_of(self.p.outer(k), self.rows)]
        return pltpu.make_async_copy(src, self.own.at[k], self.ls.at[k])

    def near(self, k, m):
        p, n = self.p, k * self.p.inner_size + m
        at = p.outer_of(k) * p.inner_size + p.inner_of(m)
        return remote(self.part.at[rows_of(at, self.rows)], self.near_got.at[n], self.s1.at[n], self.r1.at[n], "dp", p.inner(m))

    def far(self, k):
        return remote(self.mid_sum.at[k], self.far_got.at[k], self.s2.at[k], self.r2.at[k], "dp", self.p.outer(k))

    def begin(self):
        for k in list(range(1, OUTER)) + [0]:
            for m in range(1, self.p.inner_size):
                self.near(k, m).start()
            self.local(k).start()

    def near_sum(self, k):
        self.local(k).wait()
        total = self.own[k].astype(F32)
        for m in range(1, self.p.inner_size):
            self.near(k, m).wait_recv()
            total = total + self.near_got[k * self.p.inner_size + m].astype(F32)
        return total

    def mid(self):
        for k in range(1, OUTER):
            self.mid_sum[k] = self.near_sum(k).astype(BF16)
            self.far(k).start()

    def end(self):
        total = self.near_sum(0)
        for k in range(1, OUTER):
            self.far(k).wait_recv()
            total = total + self.far_got[k].astype(F32)
        return total

    def drain(self):
        for k in range(OUTER):
            for m in range(1, self.p.inner_size):
                self.near(k, m).wait_send()
            if k:
                self.far(k).wait_send()


def take(refs, counts):
    out, at = [], 0
    for count in counts:
        out.append(refs[at : at + count])
        at += count
    return out


def comm_params(number):
    return pltpu.CompilerParams(collective_id=number, has_side_effects=True)


def inverse_norm(values):
    return lax.rsqrt(jnp.mean(values * values, axis=-1, keepdims=True) + EPS)


def norm_back(values, gain, upstream):
    inverse = inverse_norm(values)
    gain_part = jnp.sum(upstream * values * inverse, axis=0, keepdims=True)
    scaled = upstream * gain
    inner = jnp.mean(scaled * values, axis=-1, keepdims=True)
    return inverse * scaled - values * (inverse * inverse * inverse * inner), gain_part


def by_rows(left, right):
    def value(rows):
        return lax.dot_general(left[rows, :], right[...], (((1,), (1,)), ((), ())), preferred_element_type=F32)

    return value


def finish_kernel(pack, gains, rates, result, in_grad, conv_sum, gate_sum, qkv_sum, out_sum, attn_sum, up_sum, down_sum,
                  o_result, o_in_grad, o_gain1, o_in, o_convw, o_convb, o_xproj, o_dtproj, o_dtb, o_alog, o_skip,
                  o_out, o_gain2, o_qkv, o_attn, o_gain3, o_up, o_down):
    at = MIX + RANK + NST
    values = pack[...].astype(F32)
    o_result[...] = result[...]
    o_in_grad[...] = in_grad[...]
    o_gain1[...] = gains[0:1, :]
    o_gain2[...] = gains[1:2, :]
    o_gain3[...] = gains[2:3, :]
    o_in[:, 0, :] = conv_sum[...]
    o_in[:, 1, :] = gate_sum[...]
    width = o_qkv.shape[2]
    for n in range(3):
        o_qkv[n] = qkv_sum[:, n * width : (n + 1) * width]
    o_convw[...] = values[at : at + KC]
    o_convb[...] = values[at + KC : at + KC + 1]
    o_xproj[...] = values[:MIX]
    o_dtproj[...] = values[MIX : MIX + RANK]
    o_dtb[...] = values[at + KC + 1 : at + KC + 2]
    o_alog[...] = values[MIX + RANK : at] * -jnp.exp(rates[...])
    o_skip[...] = values[at + KC + 2 : at + KC + 3]
    for out, total in ((o_out, out_sum), (o_attn, attn_sum), (o_up, up_sum), (o_down, down_sum)):
        out[...] = total[...]


def finish(in_shape, qkv_shape, pack, gains, alog, result, in_grad, *sums):
    chans, width = pack.shape[1], gains.shape[1]
    conv_sum, gate_sum, qkv_sum, out_sum, attn_sum, up_sum, down_sum = sums
    outs = [
        shaped(result.shape, BF16), shaped(in_grad.shape, F32), shaped((1, width), F32), shaped(in_shape, F32),
        shaped((KC, chans), F32), shaped((1, chans), F32), shaped((MIX, chans), F32), shaped((RANK, chans), F32),
        shaped((1, chans), F32), shaped((NST, chans), F32), shaped((1, chans), F32), shaped(out_sum.shape, F32),
        shaped((1, width), F32), shaped(qkv_shape, F32), shaped(attn_sum.shape, F32), shaped((1, width), F32),
        shaped(up_sum.shape, F32), shaped(down_sum.shape, F32),
    ]
    return pl.pallas_call(
        finish_kernel,
        out_shape=outs,
        in_specs=[VM] * 12,
        out_specs=[VM] * len(outs),
        name="finish",
    )(pack, gains, alog, result, in_grad, *sums)


def softplus(v):
    return jnp.maximum(v, 0.0) + jnp.log1p(jnp.exp(-jnp.abs(v)))

def dot32(a, b, dims=((1,), (0,))):
    return lax.dot_general(a, b, (dims, ((), ())), preferred_element_type=F32)

def eye_rows(rows, cols, shift):
    r = lax.broadcasted_iota(jnp.int32, (rows, cols), 0)
    c = lax.broadcasted_iota(jnp.int32, (rows, cols), 1)
    return (c == r + shift).astype(BF16)

def spread_cols(rows_low):
    n = lax.broadcasted_iota(jnp.int32, (NST, GT * NST), 0)
    col = lax.broadcasted_iota(jnp.int32, (NST, GT * NST), 1)
    wide = dot32(rows_low, (col % NST == n).astype(BF16))
    t = lax.broadcasted_iota(jnp.int32, (TB, GT * NST), 0)
    col2 = lax.broadcasted_iota(jnp.int32, (TB, GT * NST), 1)
    return jnp.where(t % GT == col2 // NST, wide, 0.0).astype(BF16)

PAD = 8


def wide(values, chans):
    return jnp.concatenate([values] * (chans // 128), axis=1)


def rows_at(start, count):
    return slice(start, start + count)


def front_kernel(tp, dp, tokens, gain, in_shard, conv_w, conv_b, xproj, seg_row, dtproj_ref, dtb_ref, alog_ref, skip_ref,
                 qkv_shard, grad_rows, out_shard, *refs):
    place = Place(tp, dp)
    ((states_ref, scanned_ref, gated_ref), kept, (grad_full, out_full, qkv_full),
     (low, conv_shard, gate_shard, qkv_flat, rows_full, in_conv, in_gate, conv_in, conv_pre, conv_low, gate_s, mixed_ref, segs,
      part_ref, h_ref, step_ref, u_ref, local_sem), row_refs, total_refs, grad_refs, conv_refs, gate_refs, out_refs, qkv_refs) = take(
        refs, (3, 9, 3, 18, 6, 7, 6, 5, 5, 5, 5)
    )
    block, blocks = pl.program_id(0), pl.num_programs(0)
    every, chans = conv_low.shape
    gather = TpGather(place, low, rows_full, row_refs)
    total = TpTotal(place, part_ref, total_refs)
    grads = TpGather(place, grad_rows, grad_full, grad_refs)
    conv_job = DpGather(place, conv_shard, in_conv, conv_refs)
    gate_job = DpGather(place, gate_shard, in_gate, gate_refs)
    later = [DpGather(place, out_shard, out_full, out_refs), DpGather(place, qkv_flat, qkv_full, qkv_refs)]
    sources = [rows_full, in_conv, in_gate, conv_in.at[pl.ds(PAD, every)], conv_pre, conv_low, gate_s, mixed_ref, segs.at[pl.ds(PAD, every)]]

    def store(n):
        return pltpu.make_async_copy(sources[n], kept[n], local_sem.at[n])

    def own_rows():
        return pltpu.make_async_copy(grad_rows, grad_full.at[rows_of(place.me, grads.rows)], local_sem.at[len(sources)])

    @pl.when(block == 0)
    def _():
        place.barrier()
        conv_shard[...] = in_shard[:, 0, :]
        conv_job.begin()
        for s in range(PARTS):
            at = pl.ds(s * (low.shape[0] // PARTS), low.shape[0] // PARTS)
            values = tokens[at, :].astype(F32)
            low[at, :] = (values * inverse_norm(values) * gain[...]).astype(BF16)
            gather.begin(s)
        gate_shard[...] = in_shard[:, 1, :]
        gate_job.begin()
        rows_full[rows_of(place.me, low.shape[0]), :] = low[...]
        width = qkv_shard.shape[2]
        for n in range(3):
            qkv_flat[:, n * width : (n + 1) * width] = qkv_shard[n]
        h_ref[...] = jnp.zeros_like(h_ref)
        conv_in[0:PAD, :] = jnp.zeros((PAD, chans), F32)
        segs[0:PAD, :] = jnp.full((PAD, 128), -1.0, F32)
        segs[PAD : PAD + every, :] = jnp.broadcast_to(seg_row[...].astype(F32), (128, every)).T
        conv_job.mid()
        gather.mid()
        gate_job.mid()
        conv_job.end()

        def project(rows):
            at = pl.ds(pl.multiple_of(rows.start + PAD, PAD), rows.size)
            conv_in[at, :] = dot32(rows_full[rows, :], in_conv[...])

        gather.each(project, False)
        for n in range(every // TB):
            seg = segs[rows_at(PAD + n * TB, TB), :]
            pre = conv_b[...] + conv_w[KC - 1 : KC, :] * conv_in[rows_at(PAD + n * TB, TB), :]
            for k in range(1, KC):
                same = (segs[rows_at(PAD + n * TB - k, TB), :] == seg).astype(F32)
                pre = pre + conv_w[KC - 1 - k : KC - k, :] * (conv_in[rows_at(PAD + n * TB - k, TB), :] * wide(same, chans))
            conv_pre[rows_at(n * TB, TB), :] = pre
            active = (pre * jax.nn.sigmoid(pre)).astype(BF16)
            conv_low[rows_at(n * TB, TB), :] = active
            part_ref[rows_at(n * TB, TB), :] = dot32(active, xproj[...], ((1,), (1,))).astype(BF16)
        total.begin()
        gate_job.end()
        for n in range(tp):
            rows = slice(n * low.shape[0], (n + 1) * low.shape[0])
            gate_s[rows, :] = dot32(rows_full[rows, :], in_gate[...])
        mixed_ref[...] = total.run().astype(BF16)
        for s in range(PARTS):
            grads.begin(s)
        for job in later:
            job.begin()
        own_rows().start()
        for n in range(len(sources)):
            store(n).start()

    for n in range(2):

        @pl.when(block == blocks * (2 * n + 3) // 8)
        def _(n=n):
            later[n].mid()

    @pl.when(block == blocks * 5 // 8)
    def _():
        grads.mid()

    here = rows_of(block, TB)
    mixed = mixed_ref[here, :]
    conv = conv_low[here, :].astype(F32)
    step = softplus(dot32(mixed[:, :RANK], dtproj_ref[...]) + dtb_ref[...])
    first = pl.multiple_of(block * TB, TB)
    near = segs[pl.ds(first, TB + PAD), :]
    cut = jnp.where(near[PAD:, :] == near[PAD - 1 : PAD - 1 + TB, :], 0.0, BIG)
    step_ref[...] = jnp.maximum(step, wide(cut, chans))
    u_ref[...] = step * conv
    b_t = dot32(eye_rows(NST, MIX, RANK), mixed, ((1,), (1,)))
    c_wide = spread_cols(mixed[:, RANK + NST :])
    rates = -LOG2E * jnp.exp(alog_ref[...])

    h = h_ref[...]
    for j in range(TB):
        decay = jnp.exp2(step_ref[j : j + 1, :] * rates)
        h = decay * h + u_ref[j : j + 1, :] * b_t[:, j : j + 1]
        states_ref[j * NST : (j + 1) * NST, :] = h.astype(BF16)
    h_ref[...] = h
    skip = skip_ref[...]
    gates = gate_s[here, :]
    for g in range(TB // GT):
        rows = slice(g * GT, (g + 1) * GT)
        y = dot32(c_wide[rows], states_ref[g * GT * NST : (g + 1) * GT * NST, :])
        y = y + skip * conv[rows]
        scanned_ref[rows, :] = y
        gate = gates[rows]
        gated_ref[rows, :] = (y * (gate * jax.nn.sigmoid(gate))).astype(BF16)

    @pl.when(block == blocks - 1)
    def _():
        grads.end()
        for job in later:
            job.end()
        own_rows().wait()
        for n in range(len(sources)):
            store(n).wait()
        for job in [gather, total, grads, conv_job, gate_job] + later:
            job.drain()


def front(tp, dp, tokens, gain, in_weight, conv_w, conv_b, xproj_t, seg_row, dtproj, dtb, alog_t, skip, qkv_t, grad_rows, out_weight):
    rows, width = tokens.shape
    shard, chans = in_weight.shape[0], in_weight.shape[2]
    every = seg_row.shape[1]
    att = qkv_t.shape[0] * qkv_t.shape[2]
    row = lambda w: pl.BlockSpec((TB, w), lambda i: (i, 0))
    whole = lambda a: pl.BlockSpec(a.shape, lambda i, n=a.ndim: (0,) * n)
    vmem = lambda shape, dtype=BF16: pltpu.VMEM(shape, dtype)
    inputs = (tokens, gain, in_weight, conv_w, conv_b, xproj_t, seg_row, dtproj, dtb, alog_t, skip, qkv_t)
    return pl.pallas_call(
        functools.partial(front_kernel, tp, dp),
        grid=(every // TB,),
        in_specs=[whole(a) for a in inputs] + [ANY] * 2,
        out_specs=[pl.BlockSpec((TB * NST, chans), lambda i: (i, 0)), row(chans), row(chans)] + [ANY] * 12,
        out_shape=[
            shaped((every * NST, chans), BF16), shaped((every, chans), F32), shaped((every, chans), BF16),
            shaped((every, width), BF16), shaped((width, chans), BF16), shaped((width, chans), BF16), shaped((every, chans), F32),
            shaped((every, chans), F32), shaped((every, chans), BF16), shaped((every, chans), F32), shaped((every, MIX), BF16),
            shaped((every, 128), F32),
            shaped((every, width), BF16), shaped((width, chans), BF16), shaped((width, att), BF16),
        ],
        scratch_shapes=[
            vmem((rows, width)), vmem((shard, chans)), vmem((shard, chans)), vmem((shard, att)), vmem((every, width)),
            vmem((width, chans)), vmem((width, chans)), vmem((PAD + every, chans), F32), vmem((every, chans), F32),
            vmem((every, chans)), vmem((every, chans), F32), vmem((every, MIX)), vmem((PAD + every, 128), F32), vmem((every, MIX)),
            vmem((NST, chans), F32), vmem((TB, chans), F32), vmem((TB, chans), F32), dma(10),
        ]
        + TpGather.scratch(tp) + TpTotal.scratch(tp, every, MIX) + TpGather.scratch(tp) + DpGather.scratch(dp) * 4,
        compiler_params=pltpu.CompilerParams(
            collective_id=2, has_side_effects=True, dimension_semantics=("arbitrary",)
        ),
        name="front",
    )(*inputs, grad_rows, out_weight)


def back_kernel(tp, dp, conv_ref, mixed_ref, gate_ref, scanned_ref, gg_ref, states_ref, prev_ref, dtproj_ref, dtb_ref,
                alog_ref, skip_ref, feed_ref, after_ref, resid, tokens, gain, gain_two, gain_three, conv_w, xproj, *refs):
    place = Place(tp, dp)
    (saved, grads, (result_ref, in_grad, conv_sum, gate_sum, pack_sum, gains), sums,
     (e_ref, step_ref, dy_ref, g_ref, w_ref, part_ref, step_low_ref, gate_grad_ref, conv_grad_ref, mixed_grad_ref, small_ref),
     loaded, (pre_ref, cig_ref, part, conv_wgrad, gate_wgrad, pack, pack_low, pack_all, g0, g1, g2, g3, gs, gr, ds, dr, local_sem),
     feed_refs, total_refs, scatter_refs, conv_refs, gate_refs, pack_refs, spread_refs, rest) = take(
        refs, (8, 3, 6, 3, 11, 8, 17, 7, 7, 7, 9, 9, 9, 5, 27)
    )
    step_id, blocks = pl.program_id(0), pl.num_programs(0)
    chans = conv_ref.shape[1]
    rows_full, in_conv, in_gate, conv_in, conv_pre, conv_low, mixed_all, segs = loaded
    every = conv_low.shape[0]
    feed = TpScatter(place, feed_ref, feed_refs)
    total = TpTotal(place, part_ref, total_refs)
    weights = [DpScatter(place, grads[n], rest[9 * n : 9 * n + 9]) for n in range(3)]
    conv_job = DpScatter(place, conv_wgrad, conv_refs)
    gate_job = DpScatter(place, gate_wgrad, gate_refs)
    small = DpScatter(place, pack, pack_refs)
    spread = DpGather(place, pack_low, pack_all, spread_refs)

    def proj_value(rows):
        return dot32(cig_ref[rows, :], in_conv[...], ((1,), (1,))) + dot32(gate_grad_ref[rows, :], in_gate[...], ((1,), (1,)))

    scatter = TpScatter(place, part, scatter_refs, proj_value)

    def target(n):
        if n == 3:
            return loaded[n].at[pl.ds(PAD, every)]
        return loaded[n].at[pl.ds(PAD, every)] if n == 7 else loaded[n]

    def load(n):
        return pltpu.make_async_copy(saved[n], target(n), local_sem.at[n])

    @pl.when(step_id == 0)
    def _():
        place.barrier(True)
        load(7).start()
        feed.begin()
        for job in weights:
            job.begin()
        for n in range(7):
            load(n).start()
        e_ref[...] = jnp.zeros_like(e_ref)
        small_ref[...] = jnp.zeros_like(small_ref)
        conv_in[0:PAD, :] = jnp.zeros((PAD, chans), F32)
        segs[0:PAD, :] = jnp.full((PAD, 128), -1.0, F32)
        segs[PAD + every :, :] = jnp.full((PAD, 128), -1.0, F32)
        pre_ref[every:, :] = jnp.zeros((PAD, chans), F32)
        load(7).wait()

    @pl.when(step_id == blocks // 4)
    def _():
        feed.mid()

    @pl.when(step_id == blocks // 2)
    def _():
        for job in weights:
            job.mid()

    block = blocks - 1 - step_id
    here = rows_of(block, TB)
    conv = conv_ref[...].astype(F32)
    mixed = mixed_ref[...]
    step_in = dot32(mixed[:, :RANK], dtproj_ref[...]) + dtb_ref[...]
    step = softplus(step_in)
    near = segs[pl.ds(pl.multiple_of(block * TB, TB), TB + PAD), :]
    cut = jnp.where(near[PAD:, :] == near[PAD - 1 : PAD - 1 + TB, :], 0.0, BIG)
    step_ref[...] = jnp.maximum(step, wide(cut, chans))
    u_low = (step * conv).astype(BF16)
    gate = gate_ref[...]
    sig = jax.nn.sigmoid(gate)
    gg = gg_ref[...]
    dy = gg * (gate * sig)
    gate_grad_ref[here, :] = (gg * scanned_ref[...] * (sig + gate * sig * (1.0 - sig))).astype(BF16)
    dy_ref[...] = dy
    small_ref[NST + 1 : NST + 2, :] += jnp.sum(dy * conv, axis=0, keepdims=True)
    c_t = dot32(eye_rows(NST, MIX, RANK + NST), mixed, ((1,), (1,)))
    b_wide = spread_cols(mixed[:, RANK : RANK + NST])
    rates = -LOG2E * jnp.exp(alog_ref[...])

    e = e_ref[...]
    acc = jnp.zeros((NST, chans), F32)
    for j in range(TB - 1, -1, -1):
        before = (prev_ref[...] if j == 0 else states_ref[(j - 1) * NST : j * NST, :]).astype(F32)
        step_row = step_ref[j : j + 1, :]
        decay = jnp.exp2(step_row * rates)
        grad = c_t[:, j : j + 1] * dy_ref[j : j + 1, :] + e
        e = decay * grad
        weighted = e * before
        acc = acc + weighted * step_row
        g_ref[j * NST : (j + 1) * NST, :] = grad.astype(BF16)
        w_ref[j * NST : (j + 1) * NST, :] = (weighted * rates).astype(BF16)
    e_ref[...] = e
    small_ref[0:NST, :] += acc
    skip = skip_ref[...]
    dy_low = dy.astype(BF16)
    ones_wide = spread_cols(jnp.ones((TB, NST), BF16))
    lane = lax.broadcasted_iota(jnp.int32, (NST, TB), 1)
    b_grad = jnp.zeros((NST, TB), F32)
    c_grad = jnp.zeros((NST, TB), F32)
    for g in range(TB // GT):
        rows = slice(g * GT, (g + 1) * GT)
        span = slice(g * GT * NST, (g + 1) * GT * NST)
        grad = g_ref[span, :]
        along_b = dot32(b_wide[rows], grad)
        step_grad = dot32(ones_wide[rows], w_ref[span, :]) * (1.0 / LOG2E) + along_b * conv[rows]
        conv_grad_ref[rows_of(block * (TB // GT) + g, GT), :] = along_b * step[rows] + skip * dy[rows]
        step_in_grad = step_grad * jax.nn.sigmoid(step_in[rows])
        small_ref[NST : NST + 1, :] += jnp.sum(step_in_grad, axis=0, keepdims=True)
        step_low_ref[rows_of(block * (TB // GT) + g, GT), :] = step_in_grad.astype(BF16)
        by_u = dot32(grad, u_low, ((1,), (1,)))
        by_dy = dot32(states_ref[span, :], dy_low, ((1,), (1,)))
        for j in range(GT):
            hit = lane == g * GT + j
            b_grad = jnp.where(hit, by_u[j * NST : (j + 1) * NST], b_grad)
            c_grad = jnp.where(hit, by_dy[j * NST : (j + 1) * NST], c_grad)
    rank_part = dot32(step_low_ref[here, :], dtproj_ref[...], ((1,), (1,)))
    state_part = jnp.concatenate([b_grad, c_grad], axis=0).T
    part_ref[here, :] = jnp.concatenate([rank_part, state_part], axis=1).astype(BF16)

    @pl.when(step_id == blocks - 1)
    def _():
        total.begin()
        for n in range(7):
            load(n).wait()
        gate_wgrad[...] = tn(rows_full[...], gate_grad_ref[...]).astype(BF16)
        gate_job.begin()
        for job, out in zip(weights, sums):
            out[...] = job.end()
        for s in range(PARTS):
            at = feed.piece(s)
            result_ref[at, :] = (after_ref[at, :] + feed.end(s)).astype(BF16)
        mixed_grad_ref[...] = total.run().astype(BF16)
        bias_sum = jnp.zeros((1, chans), F32)
        taps = [jnp.zeros((1, chans), F32) for _ in range(KC)]
        for n in range(every // TB):
            at = rows_at(n * TB, TB)
            pre = conv_pre[at, :]
            sig_pre = jax.nn.sigmoid(pre)
            grad = conv_grad_ref[at, :] + dot32(mixed_grad_ref[at, :], xproj[...])
            grad = grad * (sig_pre + pre * sig_pre * (1.0 - sig_pre))
            pre_ref[at, :] = grad
            bias_sum = bias_sum + jnp.sum(grad, axis=0, keepdims=True)
            seg = segs[rows_at(PAD + n * TB, TB), :]
            for k in range(KC):
                term = conv_in[rows_at(PAD + n * TB - k, TB), :]
                if k:
                    same = (segs[rows_at(PAD + n * TB - k, TB), :] == seg).astype(F32)
                    term = term * wide(same, chans)
                taps[KC - 1 - k] = taps[KC - 1 - k] + jnp.sum(grad * term, axis=0, keepdims=True)
        for n in range(every // TB):
            seg = segs[rows_at(PAD + n * TB, TB), :]
            grad = conv_w[KC - 1 : KC, :] * pre_ref[rows_at(n * TB, TB), :]
            for k in range(1, KC):
                same = (segs[rows_at(PAD + n * TB + k, TB), :] == seg).astype(F32)
                grad = grad + conv_w[KC - 1 - k : KC - k, :] * (pre_ref[rows_at(n * TB + k, TB), :] * wide(same, chans))
            cig_ref[rows_at(n * TB, TB), :] = grad.astype(BF16)
        scatter.begin()
        gate_job.mid()
        conv_wgrad[...] = tn(rows_full[...], cig_ref[...]).astype(BF16)
        conv_job.begin()
        scatter.mid()
        at = MIX + RANK
        pack[0:MIX, :] = tn(mixed_grad_ref[...], conv_low[...]).astype(BF16)
        pack[MIX:at, :] = tn(mixed_all[:, :RANK], step_low_ref[...]).astype(BF16)
        tail = jnp.concatenate(
            [small_ref[0:NST, :]] + taps + [bias_sum, small_ref[NST : NST + 2, :], jnp.zeros((pack.shape[0] - at - NST - KC - 3, chans), F32)], axis=0
        )
        pack[at:, :] = tail.astype(BF16)
        small.begin()
        conv_job.mid()
        gain_one = jnp.zeros(gain.shape, F32)
        for s in range(PARTS):
            at = scatter.piece(s)
            grad, gain_sum = norm_back(tokens[at, :].astype(F32), gain[...], scatter.end(s))
            in_grad[at, :] = resid[at, :] + grad
            gain_one = gain_one + gain_sum
        g0[0:1, :] = gain_one
        g0[1:2, :] = gain_two[...]
        g0[2:3, :] = gain_three[...]
        g0[3:8, :] = jnp.zeros((5, g0.shape[1]), F32)

        def pair():
            return remote(g0, g1.at[0], gs.at[0], gr.at[0], "tp", place.sibling)

        def chip(k):
            return remote(g2, g1.at[k], gs.at[k], gr.at[k], "tp", place.peer(k))

        def far(k):
            return remote(g2, g3.at[k], ds.at[k], dr.at[k], "dp", place.along(k))

        pair().start()
        small.mid()
        pair().wait_recv()
        g2[...] = g0[...] + g1[0]
        both = g2[...]
        for k in range(1, place.chips):
            chip(k).start()
        pack_low[...] = small.end().astype(BF16)
        spread.begin()
        for k in range(1, place.chips):
            chip(k).wait_recv()
            both = both + g1[k]
        for k in range(1, place.chips):
            chip(k).wait_send()
        g2[...] = both
        for k in range(1, dp):
            far(k).start()
        spread.mid()
        gate_sum[...] = gate_job.end()
        conv_sum[...] = conv_job.end()
        for k in range(1, dp):
            far(k).wait_recv()
            both = both + g3[k]
        gains[...] = both
        spread.end()
        pack_sum[...] = pack_all[...]
        pair().wait_send()
        for k in range(1, dp):
            far(k).wait_send()
        for job in [feed, total, scatter, conv_job, gate_job, small, spread] + weights:
            job.drain()


def back(tp, dp, conv_low, mixed, gate, scanned, gated_grad, states, dtproj, dtb, alog_t, skip, feed, after, resid, tokens,
         gain, gain_two, gain_three, conv_w, xproj_t, saved, grads):
    every, chans = conv_low.shape
    rows, width = resid.shape
    blocks = every // TB
    row = lambda w: pl.BlockSpec((TB, w), lambda i: (blocks - 1 - i, 0))
    fixed = lambda r, c: pl.BlockSpec((r, c), lambda i: (0, 0))
    whole = lambda a: fixed(*a.shape)
    vmem = lambda shape, dtype=BF16: pltpu.VMEM(shape, dtype)
    shards = [(grad.shape[0] // dp, grad.shape[1]) for grad in grads]
    half = (width // dp, chans)
    pack_rows = 16 * dp * (-(-(MIX + RANK + NST + KC + 3) // (16 * dp)))
    small = (pack_rows // dp, chans)
    scratch = []
    for shard in shards:
        scratch += DpScatter.scratch(dp, *shard)
    wholes = (dtproj, dtb, alog_t, skip, feed, after, resid, tokens, gain, gain_two, gain_three, conv_w, xproj_t)
    return pl.pallas_call(
        functools.partial(back_kernel, tp, dp),
        grid=(blocks,),
        in_specs=[row(chans), row(MIX), row(chans), row(chans), row(chans),
                  pl.BlockSpec((TB * NST, chans), lambda i: (blocks - 1 - i, 0)),
                  pl.BlockSpec((NST, chans), lambda i: (jnp.maximum((blocks - 1 - i) * TB - 1, 0), 0))]
        + [whole(a) for a in wholes] + [ANY] * (len(saved) + len(grads)),
        out_specs=[fixed(rows, width), fixed(rows, width), fixed(*half), fixed(*half), fixed(pack_rows, chans), fixed(8, width)]
        + [fixed(*shard) for shard in shards],
        out_shape=[
            shaped((rows, width), BF16), shaped((rows, width), F32), shaped(half, F32), shaped(half, F32),
            shaped((pack_rows, chans), BF16), shaped((8, width), F32),
        ]
        + [shaped(shard, F32) for shard in shards],
        scratch_shapes=[
            vmem((NST, chans), F32), vmem((TB, chans), F32), vmem((TB, chans), F32), vmem((TB * NST, chans)), vmem((TB * NST, chans)),
            vmem((every, MIX)), vmem((every, chans)), vmem((every, chans)), vmem((every, chans), F32), vmem((every, MIX)),
            vmem((24, chans), F32),
            vmem((every, width)), vmem((width, chans)), vmem((width, chans)), vmem((PAD + every, chans), F32), vmem((every, chans), F32),
            vmem((every, chans)), vmem((every, MIX)), vmem((every + 2 * PAD, 128), F32),
            vmem((every + PAD, chans), F32), vmem((every, chans)), vmem((every, width)), vmem((width, chans)), vmem((width, chans)),
            vmem((pack_rows, chans)), vmem(small), vmem((pack_rows, chans)), vmem((8, width), F32), vmem((tp // 2, 8, width), F32), vmem((8, width), F32),
            vmem((dp, 8, width), F32), dma(tp // 2), dma(tp // 2), dma(dp), dma(dp), dma(8),
        ]
        + TpScatter.scratch(tp, rows, width) + TpTotal.scratch(tp, every, MIX) + TpScatter.scratch(tp, rows, width)
        + DpScatter.scratch(dp, *half) * 2 + DpScatter.scratch(dp, *small) + DpGather.scratch(dp) + scratch,
        compiler_params=pltpu.CompilerParams(
            collective_id=7, has_side_effects=True, dimension_semantics=("arbitrary",)
        ),
        name="back",
    )(conv_low, mixed, gate, scanned, gated_grad, states, states, *wholes, *saved, *grads)


QB = 256
NEG = -1e30
RT2PI = math.sqrt(2.0 / math.pi)


def nn(a, b):
    return lax.dot_general(a, b, (((1,), (0,)), ((), ())), preferred_element_type=F32)


def nt(a, b):
    return lax.dot_general(a, b, (((1,), (1,)), ((), ())), preferred_element_type=F32)


def tn(a, b):
    return lax.dot_general(a, b, (((0,), (0,)), ((), ())), preferred_element_type=F32)


def flipped(values):
    return values.astype(F32).T.astype(BF16)


def head_lanes(values, h):
    lane = lax.broadcasted_iota(jnp.int32, values.shape, 1)
    return jnp.where(lane // HD == h, values, jnp.zeros_like(values))


def masked_scores(keys, queries, seg_keys, seg_query, diagonal):
    scores = nt(keys, queries)
    seen = jnp.concatenate([seg_keys] * (QB // 128), axis=1) == seg_query
    if diagonal:
        key_at = lax.broadcasted_iota(jnp.int32, scores.shape, 0)
        query_at = lax.broadcasted_iota(jnp.int32, scores.shape, 1)
        seen = seen & (key_at <= query_at)
    return jnp.where(seen, scores, NEG)


def attend(qkv, seg_col, seg_row, flip, out, totals):
    tokens, width = out.shape
    heads = width // HD
    for q in range(tokens // LEN):
        base = q * LEN
        flip[...] = flipped(qkv[base : base + LEN, 2 * width :])
        for i in range(LEN // QB):
            at = slice(base + i * QB, base + (i + 1) * QB)
            queries = (qkv[at, :width].astype(F32) * (1.0 / math.sqrt(HD))).astype(BF16)
            columns = []
            for h in range(heads):
                own = head_lanes(queries, h)
                parts = []
                for j in range(i + 1):
                    to = slice(base + j * QB, base + (j + 1) * QB)
                    parts.append(masked_scores(qkv[to, width : 2 * width], own, seg_col[to, :], seg_row[:, at].astype(F32), j == i))
                peak = functools.reduce(jnp.maximum, [jnp.max(part, axis=0, keepdims=True) for part in parts])
                total, mixed = jnp.zeros_like(peak), jnp.zeros((HD, QB), F32)
                for j, part in enumerate(parts):
                    weight = jnp.exp(part - peak)
                    total = total + jnp.sum(weight, axis=0, keepdims=True)
                    mixed = mixed + nn(flip[h * HD : (h + 1) * HD, j * QB : (j + 1) * QB], weight.astype(BF16))
                totals[q * heads + h : q * heads + h + 1, i * QB : (i + 1) * QB] = peak + jnp.log(total)
                columns.append(mixed / total)
            out[at, :] = jnp.concatenate(columns, axis=0).T.astype(BF16)


def attend_back(qkv, grad, seg_col, seg_row, totals, flip, key_grad, value_grad, out):
    tokens, width = grad.shape
    heads = width // HD
    scale = 1.0 / math.sqrt(HD)
    for q in range(tokens // LEN):
        base = q * LEN
        flip[...] = flipped(qkv[base : base + LEN, width : 2 * width])
        for i in range(LEN // QB):
            at = slice(base + i * QB, base + (i + 1) * QB)
            queries = (qkv[at, :width].astype(F32) * scale).astype(BF16)
            columns = []
            for h in range(heads):
                own, own_grad = head_lanes(queries, h), head_lanes(grad[at, :], h)
                log_total = totals[q * heads + h : q * heads + h + 1, i * QB : (i + 1) * QB]
                inner = jnp.zeros((1, QB), F32)
                probs, prob_grads = [], []
                for j in range(i + 1):
                    to = slice(base + j * QB, base + (j + 1) * QB)
                    scores = masked_scores(qkv[to, width : 2 * width], own, seg_col[to, :], seg_row[:, at].astype(F32), j == i)
                    prob = jnp.exp(scores - log_total)
                    prob_grad = nt(qkv[to, 2 * width :], own_grad)
                    inner = inner + jnp.sum(prob * prob_grad, axis=0, keepdims=True)
                    probs.append(prob)
                    prob_grads.append(prob_grad)
                query_grad = jnp.zeros((HD, QB), F32)
                for j in range(i + 1):
                    rows = slice(j * QB, (j + 1) * QB)
                    score_grad = (probs[j] * (prob_grads[j] - inner)).astype(BF16)
                    add_key = nn(score_grad, own)
                    add_value = nn(probs[j].astype(BF16), own_grad)
                    if i == j and h == 0:
                        key_grad[rows, :] = add_key
                        value_grad[rows, :] = add_value
                    else:
                        key_grad[rows, :] += add_key
                        value_grad[rows, :] += add_value
                    query_grad = query_grad + nn(flip[h * HD : (h + 1) * HD, rows], score_grad)
                columns.append(query_grad)
            out[at, :width] = (jnp.concatenate(columns, axis=0).T * scale).astype(BF16)
        out[base : base + LEN, width : 2 * width] = key_grad[...].astype(BF16)
        out[base : base + LEN, 2 * width :] = value_grad[...].astype(BF16)


def gelu_pair(v):
    square = v * v
    t = jnp.tanh(RT2PI * (v + 0.044715 * (square * v)))
    half = 0.5 * (1.0 + t)
    return v * half, half + (0.5 * RT2PI) * v * (1.0 - t * t) * (1.0 + (3.0 * 0.044715) * square)


def middle_kernel(tp, dp, gated, out_full, tokens, gain_two, gain_three, qkv_full, feed_rows, out_grad, seg_col, seg_row,
                  attn_shard, up_shard, down_shard, *refs):
    place = Place(tp, dp)
    ((stream, part_two, part_three, gated_grad, out_wgrad, attn_wgrad, qkv_wgrad, feed, after_attn, up_sum, down_sum),
     (attn_full, up_full, down_full, low, part, after_mixer, attn_rows, ffn_rows, branch_rows, qkv, attended, hidden, up_grad,
      attn_stream, att_grad, qkv_grad, up_wgrad, down_wgrad, totals, flip, key_grad, value_grad, wgrad),
     attn_refs, up_refs, down_refs, upg_refs, downg_refs, sc1, sc2, sc3, sc4, ga1, ga2, ga3, ga4) = take(
        refs, (11, 23, 5, 5, 5, 9, 9, 7, 7, 7, 7, 6, 6, 6, 6)
    )
    shards = [
        DpGather(place, attn_shard, attn_full, attn_refs),
        DpGather(place, up_shard, up_full, up_refs),
        DpGather(place, down_shard, down_full, down_refs),
    ]
    grads = [DpScatter(place, down_wgrad, downg_refs), DpScatter(place, up_wgrad, upg_refs)]
    started = []

    def scatter_of(left, right, refs):
        job = TpScatter(place, part, refs, by_rows(left, right))
        started.append(job)
        job.begin()
        return job

    def gather_of(full, refs):
        job = TpGather(place, low, full, refs)
        started.append(job)
        return job

    def settle():
        for job in started:
            job.drain()
        started.clear()

    def keep_own(full):
        full[rows_of(place.me, low.shape[0]), :] = low[...]

    place.barrier()
    scatter = scatter_of(gated, out_full, sc1)
    for job in shards:
        job.begin()
    scatter.mid()
    gather = gather_of(attn_rows, ga1)
    for s in range(PARTS):
        at = scatter.piece(s)
        values = tokens[at, :].astype(F32) + scatter.end(s)
        after_mixer[at, :] = values
        low[at, :] = (values * inverse_norm(values) * gain_two[...]).astype(BF16)
        gather.begin(s)
    keep_own(attn_rows)

    def project(rows):
        qkv[rows, :] = nn(attn_rows[rows, :], qkv_full[...]).astype(BF16)

    gather.each(project)
    settle()
    for job in shards:
        job.mid()
    attend(qkv, seg_col, seg_row, flip, attended, totals)
    shards[0].end()
    scatter = scatter_of(attended, attn_full, sc2)
    scatter.mid()
    gather = gather_of(ffn_rows, ga2)
    for s in range(PARTS):
        at = scatter.piece(s)
        values = after_mixer[at, :] + scatter.end(s)
        after_attn[at, :] = values
        low[at, :] = (values * inverse_norm(values) * gain_three[...]).astype(BF16)
        gather.begin(s)
    keep_own(ffn_rows)
    shards[1].end()
    shards[2].end()

    def feed_forward(rows):
        active, slope = gelu_pair(nn(ffn_rows[rows, :], up_full[...]))
        hidden[rows, :] = active.astype(BF16)
        up_grad[rows, :] = (nn(feed_rows[rows, :], down_full[...]) * slope).astype(BF16)

    gather.each(feed_forward)
    settle()
    scatter = scatter_of(up_grad, up_full, sc3)
    scatter.mid()
    down_wgrad[...] = tn(feed_rows[...], hidden[...]).astype(BF16)
    up_wgrad[...] = tn(ffn_rows[...], up_grad[...]).astype(BF16)
    gather = gather_of(branch_rows, ga3)
    gain_total = jnp.zeros(part_three.shape, F32)
    for s in range(PARTS):
        at = scatter.piece(s)
        back, gain_sum = norm_back(after_attn[at, :], gain_three[...], scatter.end(s))
        total = out_grad[at, :].astype(F32) + back
        low[at, :] = total.astype(BF16)
        gather.begin(s)
        attn_stream[at, :] = total
        gain_total = gain_total + gain_sum
    part_three[...] = gain_total
    keep_own(branch_rows)
    for job in grads:
        job.begin()

    def attended_back(rows):
        att_grad[rows, :] = nn(branch_rows[rows, :], attn_full[...]).astype(BF16)
        feed[rows, :] = nt(hidden[rows, :], down_full[...]).astype(BF16)

    gather.each(attended_back)
    settle()
    attend_back(qkv, att_grad, seg_col, seg_row, totals, flip, key_grad, value_grad, qkv_grad)
    scatter = scatter_of(qkv_grad, qkv_full, sc4)
    scatter.mid()
    for job in grads:
        job.mid()
    attn_wgrad[...] = tn(branch_rows[...], attended[...]).astype(BF16)
    qkv_wgrad[...] = tn(attn_rows[...], qkv_grad[...]).astype(BF16)
    gather = gather_of(ffn_rows, ga4)
    gain_total = jnp.zeros(part_two.shape, F32)
    for s in range(PARTS):
        at = scatter.piece(s)
        back, gain_sum = norm_back(after_mixer[at, :], gain_two[...], scatter.end(s))
        total = attn_stream[at, :] + back
        low[at, :] = total.astype(BF16)
        gather.begin(s)
        stream[at, :] = total
        gain_total = gain_total + gain_sum
    part_two[...] = gain_total
    keep_own(ffn_rows)
    wgrad[...] = jnp.zeros_like(wgrad)

    def gated_back(rows):
        gated_grad[rows, :] = nn(ffn_rows[rows, :], out_full[...])
        wgrad[...] += tn(ffn_rows[rows, :], gated[rows, :])

    gather.each(gated_back)
    out_wgrad[...] = wgrad[...].astype(BF16)
    down_sum[...] = grads[0].end()
    up_sum[...] = grads[1].end()
    settle()
    for job in shards + grads:
        job.drain()


def middle(tp, dp, gated, out_full, tokens, gain_two, gain_three, qkv_full, feed_rows, out_grad, seg_col, seg_row, attn_shard, up_shard, down_shard):
    rows, width = tokens.shape
    every, chans = gated.shape
    att = qkv_full.shape[1] // 3
    units = up_shard.shape[1]
    shard = up_shard.shape[0]
    vmem = lambda shape, dtype=BF16: pltpu.VMEM(shape, dtype)
    return pl.pallas_call(
        functools.partial(middle_kernel, tp, dp),
        out_shape=[
            shaped((rows, width), F32), shaped((1, width), F32), shaped((1, width), F32), shaped((every, chans), F32),
            shaped((width, chans), BF16), shaped((width, att), BF16), shaped((width, 3 * att), BF16), shaped((every, width), BF16),
            shaped((rows, width), F32), shaped((shard, units), F32), shaped((shard, units), F32),
        ],
        in_specs=[VM] * 10 + [ANY] * 3,
        out_specs=[VM] * 11,
        scratch_shapes=[
            vmem((width, att)), vmem((width, units)), vmem((width, units)), vmem((rows, width)), vmem((every, width)),
            vmem((rows, width), F32), vmem((every, width)), vmem((every, width)), vmem((every, width)), vmem((every, 3 * att)),
            vmem((every, att)), vmem((every, units)), vmem((every, units)), vmem((rows, width), F32), vmem((every, att)),
            vmem((every, 3 * att)), vmem((width, units)), vmem((width, units)), vmem((every // LEN * (att // HD), LEN), F32),
            vmem((att, LEN)), vmem((LEN, att), F32), vmem((LEN, att), F32), vmem((width, chans), F32),
        ]
        + DpGather.scratch(dp) * 3 + DpScatter.scratch(dp, shard, units) * 2
        + TpScatter.scratch(tp, rows, width) * 4 + TpGather.scratch(tp) * 4,
        compiler_params=comm_params(3),
        name="middle",
    )(gated, out_full, tokens, gain_two, gain_three, qkv_full, feed_rows, out_grad, seg_col, seg_row, attn_shard, up_shard, down_shard)


def body(
    tp,
    dp,
    tokens,
    segment_ids,
    out_grad,
    norm1_gain,
    in_weight,
    conv_weight,
    conv_bias,
    xproj_weight,
    dtproj_weight,
    dt_bias,
    a_log,
    d_skip,
    out_weight,
    norm2_gain,
    qkv_weight,
    attn_out_weight,
    norm3_gain,
    up_weight,
    down_weight,
):
    seg_row, alog_t, xproj_t = segment_ids[None], a_log.T, xproj_weight.T
    qkv_t = qkv_weight.transpose(1, 0, 2)
    (states, scanned, gated_low, mamba_rows, in_conv, in_gate, conv_in, conv_pre, conv_low, gate, mixed, segs, feed_rows,
     out_full, qkv_full) = front(
        tp, dp, tokens, norm1_gain[None], in_weight, conv_weight, conv_bias[None], xproj_t, seg_row, dtproj_weight, dt_bias[None],
        alog_t, d_skip[None], qkv_t, out_grad, out_weight,
    )
    (stream, gain_two, gain_three, gated_grad, out_grads, attn_grads, qkv_grads, feed, after_attn, up_sum, down_sum) = middle(
        tp, dp, gated_low, out_full, tokens, norm2_gain[None], norm3_gain[None], qkv_full, feed_rows, out_grad,
        segs, seg_row, attn_out_weight, up_weight, down_weight,
    )
    result, input_grad, conv_sum, gate_sum, pack_sum, gains, qkv_sum, out_sum, attn_sum = back(
        tp, dp, conv_low, mixed, gate, scanned, gated_grad, states, dtproj_weight, dt_bias[None], alog_t, d_skip[None], feed, after_attn,
        stream, tokens, norm1_gain[None], gain_two, gain_three, conv_weight, xproj_t,
        [mamba_rows, in_conv, in_gate, conv_in, conv_pre, conv_low, mixed, segs], [qkv_grads, out_grads, attn_grads],
    )
    outs = finish(
        in_weight.shape, qkv_t.shape, pack_sum, gains, alog_t, result, input_grad, conv_sum, gate_sum, qkv_sum, out_sum, attn_sum,
        up_sum, down_sum,
    )
    outs = [out[0] if out.shape[0] == 1 else out for out in outs]
    outs[6], outs[9], outs[13] = outs[6].T, outs[9].T, outs[13].transpose(1, 0, 2)
    return tuple(outs)


def solution(mesh):
    return jax.shard_map(
        functools.partial(body, mesh.shape["tp"], mesh.shape["dp"]),
        mesh=mesh,
        in_specs=(
            P(("dp", "tp"), None),
            P("dp"),
            P(("dp", "tp"), None),
            P(),
            P("dp", None, "tp"),
            P(None, "tp"),
            P("tp"),
            P("tp", None),
            P(None, "tp"),
            P("tp"),
            P("tp", None),
            P("tp"),
            P("dp", "tp"),
            P(),
            P("dp", None, "tp"),
            P("dp", "tp"),
            P(),
            P("dp", "tp"),
            P("dp", "tp"),
        ),
        out_specs=(
            P(("dp", "tp"), None),
            P(("dp", "tp"), None),
            P(),
            P("dp", None, "tp"),
            P(None, "tp"),
            P("tp"),
            P("tp", None),
            P(None, "tp"),
            P("tp"),
            P("tp", None),
            P("tp"),
            P("dp", "tp"),
            P(),
            P("dp", None, "tp"),
            P("dp", "tp"),
            P(),
            P("dp", "tp"),
            P("dp", "tp"),
        ),
        check_vma=False,
    )
```
